128 devices in a mesh: shard: 32 (over y, x, core), tensor: 4 (over z).
Axes of the slice: x: 4, y: 4, z: 4, core: 2. Of those that a mesh axis runs over, the one named last changes fastest.
Arguments:
- grads: bfloat16 [16384, 2048], P('shard', 'tensor'), may hold values from -120 to 120
- assignment: int32 [4, 32], P('tensor'), may hold values from 0 to 31, as said below
- moment: float32 [32, 2048, 512], P('shard', 'tensor'), may hold values from -6 to 6
- second: float32 [32, 2048, 512], P('shard', 'tensor'), may hold values from 0.2 to 2
- left_stats: float32 [32, 2048, 512], P('shard', 'tensor'), may hold values from -0.02 to 3.1, as said below
- right_stats: float32 [32, 2048, 512], P('shard', 'tensor'), may hold values from -0.02 to 3.1, as said below
- left_basis: float32 [32, 2048, 512], P('shard', 'tensor'), may hold values from -0.25 to 0.25
- right_basis: float32 [32, 2048, 512], P('shard', 'tensor'), may hold values from -0.25 to 0.25
Outputs:
- update: bfloat16 [16384, 2048], P('shard', 'tensor')
- new_moment: float32 [32, 2048, 512], P('shard', 'tensor')
- new_second: float32 [32, 2048, 512], P('shard', 'tensor')
- new_left_stats: float32 [32, 2048, 512], P('shard', 'tensor')
- new_right_stats: float32 [32, 2048, 512], P('shard', 'tensor')
- new_left_basis: float32 [32, 2048, 512], P('shard', 'tensor')
- new_right_basis: float32 [32, 2048, 512], P('shard', 'tensor')
The draws below stay inside these ranges and needn't reach their ends.
Inputs may be any that keep to these rules, and one draw needn't show every extreme that they name: `assignment`: within each block column the slots are distinct; slot a lies on index a // 1 of shard as its slot a % 1; in every block column some index of shard holds 1 block. `left_stats`: statistics carried from earlier steps. `right_stats`: statistics carried from earlier steps.
All inputs are finite; a program needn't handle non-finite values.
Results may differ from the reference program's by a relative error of at most 0.0004.
Values may be sent and summed in bfloat16 or wider, within the bound.
No kernel may reach another device: no remote copies, remote signals or barrier semaphores. Data moves between devices by JAX's collectives and lax.ppermute only.
A program may use at most 128 MiB of HBM per device.

```python
import math
import jax
import jax.numpy as jnp
from jax import lax

D = 2048
BLOCK = 512
SLOTS = 1
NS_ITERS = 2
ROWS = 16384
OWNER_SLOTS = 32


def draw_grads(key, part):
    key_base = jax.random.fold_in(key, 3)
    key_noise, key_rows, key_columns = jax.random.split(key_base, 3)
    row_position = jnp.arange(ROWS, dtype=jnp.float32) / ROWS
    row_scale = 10.0 ** (jax.random.uniform(key_rows, (ROWS,), jnp.float32) - 0.5)
    column_scale = 10.0 ** (jax.random.uniform(key_columns, (D,), jnp.float32) - 0.5)
    entries = jnp.clip(jax.random.normal(key_noise, (ROWS, D), jnp.float32), -4.0, 4.0)
    row_trend = jnp.exp(0.5 * math.log(3.0) * row_position)
    scaled = entries * (row_trend * row_scale)[:, None] * column_scale[None, :]
    return scaled.astype(jnp.bfloat16)


def draw_assignment(key, part):
    key_base = jax.random.fold_in(key, 5)
    owner_count = OWNER_SLOTS // SLOTS
    column_count = D // BLOCK

    def one_column(column_key):
        key_scores, key_chosen, key_order = jax.random.split(column_key, 3)
        scores = jax.random.permutation(key_scores, OWNER_SLOTS).astype(jnp.int32)
        chosen = jax.random.randint(key_chosen, (), 0, owner_count, dtype=jnp.int32)
        scores = scores.at[OWNER_SLOTS - 1].set(-1 - SLOTS)
        forced = chosen * SLOTS + jnp.arange(SLOTS, dtype=jnp.int32)
        scores = scores.at[forced].set(jnp.arange(SLOTS, dtype=jnp.int32) - SLOTS)
        ranked = jnp.argsort(scores, stable=True)[:owner_count].astype(jnp.int32)
        shuffle = jax.random.permutation(key_order, owner_count)
        return ranked[shuffle]
    column_keys = jax.random.split(key_base, column_count)
    return jax.vmap(one_column)(column_keys).astype(jnp.int32)


def statistics_draw(key):
    column_count = D // BLOCK
    key_noise, key_diagonal = jax.random.split(key)
    shape = (OWNER_SLOTS, column_count, BLOCK, BLOCK)
    noise = jnp.clip(jax.random.normal(key_noise, shape, jnp.float32), -4.0, 4.0) * 0.002
    diagonal = jnp.exp(jax.random.uniform(key_diagonal, (OWNER_SLOTS, column_count, BLOCK), jnp.float32, math.log(0.2), math.log(2.0)))
    symmetric = 0.5 * (noise + jnp.swapaxes(noise, 2, 3))
    identity_mask = (jnp.arange(BLOCK)[:, None] == jnp.arange(BLOCK)[None, :]).astype(jnp.float32)
    result = symmetric + identity_mask * diagonal[:, :, :, None]
    return result.reshape(OWNER_SLOTS, D, BLOCK).astype(jnp.float32)


def draw_left_stats(key, part):
    return statistics_draw(jax.random.fold_in(key, 11))


def draw_right_stats(key, part):
    return statistics_draw(jax.random.fold_in(key, 23))


def block_levels(key, dims, pieces, low, largest):
    def one(axis_at, blocks):
        draws = jax.random.uniform(jax.random.fold_in(jax.random.fold_in(key, 6), axis_at), (blocks,), jnp.float32, low / len(pieces), largest / len(pieces))
        return jnp.repeat(jnp.exp(draws), dims[axis_at] // blocks).reshape((-1,) + (1,) * (len(dims) - axis_at - 1))

    factor_of = one(*pieces[0])
    for cut in pieces[1:]:
        factor_of = factor_of * one(*cut)
    return factor_of


def normal_values(key, extent, scale, most, cuts=(), held_as=jnp.bfloat16):
    values = scale * jax.random.normal(key, extent, jnp.float32)
    if cuts:
        values = values * block_levels(key, extent, cuts, -0.22, 0.18)
    return jnp.clip(values, -most, most).astype(held_as)


def setup_inputs(seed: int = 0) -> dict:
    streams_of = jax.random.split(jax.random.key(seed), 9)
    grads = draw_grads(jax.random.fold_in(streams_of[8], 71), 0)
    assignment = draw_assignment(jax.random.fold_in(streams_of[8], 71), 0)
    moment = normal_values(streams_of[2], (OWNER_SLOTS, D, BLOCK), 1.0, 6.0, ((0, 32), (1, 4)), jnp.float32)
    second = jnp.clip(jnp.exp(math.log(2.0) - 2.3025851 * jax.random.uniform(streams_of[3], (OWNER_SLOTS, D, BLOCK), jnp.float32) ** block_levels(streams_of[3], (OWNER_SLOTS, D, BLOCK), ((0, 32), (1, 4)), -0.2, 0.2)), 0.2, 2.0)
    left_stats = draw_left_stats(jax.random.fold_in(streams_of[8], 71), 0)
    right_stats = draw_right_stats(jax.random.fold_in(streams_of[8], 71), 0)
    left_basis = normal_values(streams_of[6], (OWNER_SLOTS, D, BLOCK), BLOCK ** -0.5, 0.25, ((0, 32), (1, 4)), jnp.float32)
    right_basis = normal_values(streams_of[7], (OWNER_SLOTS, D, BLOCK), BLOCK ** -0.5, 0.25, ((0, 32), (1, 4)), jnp.float32)
    return {"grads": grads, "assignment": assignment, "moment": moment, "second": second, "left_stats": left_stats, "right_stats": right_stats, "left_basis": left_basis, "right_basis": right_basis}


BETA_MOMENT = 0.9
BETA_SECOND = 0.9
BETA_STATS = 0.9
ADAM_EPSILON = 1e-08
CLIP_RMS = 1.0
QUINTIC_A = 3.4445
QUINTIC_B = -4.775
QUINTIC_C = 2.0315

def highest_dot(left_side, right_side):
    return jnp.dot(left_side, right_side, precision=lax.Precision.HIGHEST, preferred_element_type=jnp.float32)

def orthonormal(product):
    iterate = product * lax.rsqrt(jnp.sum(product * product) + 1e-12)
    for sweep in range(NS_ITERS):
        gram_matrix = highest_dot(iterate.T, iterate)
        polynomial = QUINTIC_B * gram_matrix + QUINTIC_C * highest_dot(gram_matrix, gram_matrix)
        iterate = QUINTIC_A * iterate + highest_dot(iterate, polynomial)
    return iterate

def tile_update(grad_tile, factor, moment, second, left_old, right_old, left_rot, right_rot):
    block_size = grad_tile.shape[0]
    grad_float = grad_tile.astype(jnp.float32) * factor
    scale_stats = (1.0 - BETA_STATS) * factor * factor / block_size
    left_new = BETA_STATS * left_old + scale_stats * jnp.dot(grad_tile, grad_tile.T, preferred_element_type=jnp.float32)
    right_new = BETA_STATS * right_old + scale_stats * jnp.dot(grad_tile.T, grad_tile, preferred_element_type=jnp.float32)
    moment_new = BETA_MOMENT * moment + (1.0 - BETA_MOMENT) * grad_float
    rotated = highest_dot(highest_dot(left_rot.T, grad_float), right_rot)
    rotated_moment = highest_dot(highest_dot(left_rot.T, moment_new), right_rot)
    second_new = BETA_SECOND * second + (1.0 - BETA_SECOND) * rotated * rotated
    direction = rotated_moment / (jnp.sqrt(second_new) + ADAM_EPSILON)
    update = highest_dot(highest_dot(left_rot, direction), right_rot.T).astype(jnp.bfloat16)
    left_basis_new = orthonormal(highest_dot(left_old, left_rot))
    right_basis_new = orthonormal(highest_dot(right_old, right_rot))
    return (update, moment_new, second_new, left_new, right_new, left_basis_new, right_basis_new)

def reference(grads, assignment, moment, second, left_stats, right_stats, left_basis, right_basis):
    grad_float = grads.astype(jnp.float32)
    energy = jnp.sum(grad_float * grad_float)
    factor = jnp.minimum(1.0, CLIP_RMS / jnp.sqrt(energy / (ROWS * D) + 1e-12))
    block_rows = ROWS // BLOCK
    column_count = D // BLOCK
    updates = jnp.zeros((ROWS, D), jnp.bfloat16)
    zero_index = jnp.zeros((), jnp.int32)

    def visit(carry, flat_index):
        updates_now = carry[0]
        states = carry[1:]
        column = (flat_index // block_rows).astype(jnp.int32)
        tile_row = (flat_index % block_rows).astype(jnp.int32)
        slot_id = assignment[column, tile_row].astype(jnp.int32)
        row_start = (tile_row * BLOCK).astype(jnp.int32)
        column_start = (column * BLOCK).astype(jnp.int32)
        grad_tile = lax.dynamic_slice(grads, (row_start, column_start), (BLOCK, BLOCK))
        olds = tuple((lax.dynamic_slice(state, (slot_id, column_start, zero_index), (1, BLOCK, BLOCK))[0] for state in states))
        results = tile_update(grad_tile, factor, *olds)
        updates_now = lax.dynamic_update_slice(updates_now, results[0], (row_start, column_start))
        states = tuple((lax.dynamic_update_slice(state, fresh[None], (slot_id, column_start, zero_index)) for state, fresh in zip(states, results[1:])))
        return ((updates_now,) + states, None)
    start = (updates, moment, second, left_stats, right_stats, left_basis, right_basis)
    final, unused = lax.scan(visit, start, jnp.arange(block_rows * column_count, dtype=jnp.int32))
    return (final[0], final[1], final[2], final[3], final[4], final[5], final[6])
```

```python
import jax
import jax.numpy as jnp
from jax import lax
from jax.experimental import pallas as pl
from jax.experimental.pallas import tpu as pltpu
from jax.sharding import PartitionSpec as P

NS_ITERS = 2

BETA_MOMENT = 0.9
BETA_SECOND = 0.9
BETA_STATS = 0.9
ADAM_EPSILON = 1e-08
CLIP_RMS = 1.0
QUINTIC_A = 3.4445
QUINTIC_B = -4.775
QUINTIC_C = 2.0315

EXTRA = 8


def dot3(left_side, right_side):
    return jnp.dot(
        left_side, right_side, precision=lax.Precision.HIGH, preferred_element_type=jnp.float32
    )


def dot6(left_side, right_side):
    return jnp.dot(
        left_side, right_side, precision=lax.Precision.HIGHEST, preferred_element_type=jnp.float32
    )


def orthonormal(product):
    iterate = product * lax.rsqrt(jnp.sum(product * product) + 1e-12)
    for sweep in range(NS_ITERS):
        gram_matrix = dot3(iterate.T, iterate)
        polynomial = QUINTIC_B * gram_matrix + QUINTIC_C * dot3(gram_matrix, gram_matrix)
        iterate = QUINTIC_A * iterate + dot3(iterate, polynomial)
    return iterate


def forward_kernel(slots_ref, own_ref, other_ref, energy_ref, out_ref):
    rows = own_ref.shape[1]
    core = lax.rem(lax.axis_index("shard"), 2)
    for i in range(2 * own_ref.shape[0]):
        slot = slots_ref[0, i]
        chip = slot // 2
        mine = lax.rem(slot, 2) == core

        @pl.when(mine & (core == i % 2))
        def _():
            out_ref[chip, :rows, :] = own_ref[i // 2]

        @pl.when(mine & (core != i % 2))
        def _():
            out_ref[chip, :rows, :] = other_ref[i // 2]

    energy = energy_ref[...]
    high = energy.astype(jnp.bfloat16)
    rest = energy - high.astype(jnp.float32)
    middle = rest.astype(jnp.bfloat16)
    low = (rest - middle.astype(jnp.float32)).astype(jnp.bfloat16)
    row = lax.broadcasted_iota(jnp.int32, energy.shape, 0)
    packed = jnp.where(
        row == 0,
        high.astype(jnp.float32),
        jnp.where(row == 1, middle.astype(jnp.float32), low.astype(jnp.float32)),
    )
    packed = jnp.where(row < 3, packed, 0.0).astype(jnp.bfloat16)
    for chip in range(own_ref.shape[0]):
        out_ref[chip, rows:, :] = packed


def backward_kernel(slots_ref, own_ref, other_ref, out_ref):
    core = lax.rem(lax.axis_index("shard"), 2)
    for i in range(own_ref.shape[0]):
        slot = slots_ref[0, 2 * i + core]
        chip = slot // 2
        mine = lax.rem(slot, 2) == core

        @pl.when(mine)
        def _():
            out_ref[i] = own_ref[chip]

        @pl.when(jnp.logical_not(mine))
        def _():
            out_ref[i] = other_ref[chip]


def local_call(kernel, out_shape, operands):
    specs = [pl.BlockSpec(memory_space=pltpu.SMEM)]
    specs += [pl.BlockSpec(memory_space=pltpu.VMEM)] * (len(operands) - 1)
    return pl.pallas_call(
        kernel,
        out_shape=out_shape,
        in_specs=specs,
        out_specs=pl.BlockSpec(memory_space=pltpu.VMEM),
        compiler_params=pltpu.CompilerParams(vmem_limit_bytes=8 << 20),
        cost_estimate=pl.CostEstimate(flops=0, bytes_accessed=1 << 21, transcendentals=0),
    )(*operands)


def shards(grads, assignment, moment, second, left_stats, right_stats, left_basis, right_basis):
    shard_count = lax.axis_size("shard")
    tensor_count = lax.axis_size("tensor")
    size = grads.shape[1]
    chips = shard_count // 2
    rows = size // chips
    entries = size * size * shard_count * tensor_count
    same_core = [[2 * p + q for p in range(chips)] for q in range(2)]
    swap = [(i, i ^ 1) for i in range(shard_count)]

    def exchange(pieces):
        return lax.all_to_all(pieces, "shard", 0, 0, axis_index_groups=same_core)

    with jax.named_scope("spread"):
        arrived = exchange(grads.reshape(chips, rows, size))

    with jax.named_scope("energy"):
        grad_float = grads.astype(jnp.float32)
        energy = jnp.full((EXTRA, size), jnp.sum(grad_float * grad_float))
        energy = energy[:, :128]
        moved = [
            lax.ppermute(
                energy, "tensor", [(i, (i + s) % tensor_count) for i in range(tensor_count)]
            )
            for s in range(1, tensor_count)
        ]
        for part in moved:
            energy = energy + part
        energy = energy + lax.ppermute(energy, "shard", swap)
        energy = jnp.tile(energy, (1, size // 128))

    with jax.named_scope("route"):
        other = lax.ppermute(arrived, "shard", swap)
        routed = local_call(
            forward_kernel,
            jax.ShapeDtypeStruct((chips, rows + EXTRA, size), jnp.bfloat16),
            (assignment, arrived, other, energy),
        )
        gathered = exchange(routed)

    moment, second = moment[0], second[0]
    left_stats, right_stats = left_stats[0], right_stats[0]
    left_rot, right_rot = left_basis[0], right_basis[0]

    with jax.named_scope("bases"):
        left_basis_new = orthonormal(dot3(left_stats, left_rot))
        right_basis_new = orthonormal(dot3(right_stats, right_rot))
        moment_rotated = dot6(dot6(left_rot.T, moment), right_rot)

    with jax.named_scope("step"):
        packed = gathered[:, rows : rows + 3, 0].astype(jnp.float32)
        total = jnp.sum(packed)
        factor = jnp.minimum(1.0, CLIP_RMS / jnp.sqrt(total / entries + 1e-12))
        tile = gathered[:, :rows, :].reshape(size, size)
        turned = dot6(dot6(left_rot.T, tile.astype(jnp.float32)), right_rot)
        rotated = factor * turned
        rotated_moment = BETA_MOMENT * moment_rotated + (1.0 - BETA_MOMENT) * rotated
        second_new = BETA_SECOND * second + (1.0 - BETA_SECOND) * rotated * rotated
        direction = rotated_moment / (jnp.sqrt(second_new) + ADAM_EPSILON)
        update = dot6(dot6(left_rot, direction), right_rot.T).astype(jnp.bfloat16)

    with jax.named_scope("home"):
        back = exchange(update.reshape(chips, rows, size))
        other = lax.ppermute(back, "shard", swap)
        returned = local_call(
            backward_kernel,
            jax.ShapeDtypeStruct((chips, rows, size), jnp.bfloat16),
            (assignment, back, other),
        )
        update_out = exchange(returned).reshape(size, size)

    with jax.named_scope("state"):
        moment_new = BETA_MOMENT * moment + (1.0 - BETA_MOMENT) * (
            factor * tile.astype(jnp.float32)
        )
        scale_stats = (1.0 - BETA_STATS) * factor * factor / size
        left_new = BETA_STATS * left_stats + scale_stats * jnp.dot(
            tile, tile.T, preferred_element_type=jnp.float32
        )
        right_new = BETA_STATS * right_stats + scale_stats * jnp.dot(
            tile.T, tile, preferred_element_type=jnp.float32
        )

    states = (moment_new, second_new, left_new, right_new, left_basis_new, right_basis_new)
    return (update_out,) + tuple(state[None] for state in states)


def solution(mesh):
    weights = P("shard", "tensor")
    state = P("shard", "tensor", None)
    return jax.shard_map(
        shards,
        mesh=mesh,
        in_specs=(weights, P("tensor", None)) + (state,) * 6,
        out_specs=(weights,) + (state,) * 6,
        check_vma=False,
    )
```

```python
import functools
import jax
import jax.numpy as jnp
from jax import lax
from jax.experimental import pallas as pl
from jax.experimental.pallas import tpu as pltpu
from jax.sharding import PartitionSpec as P


NS_ITERS = 2
BETA_MOMENT = 0.9
BETA_SECOND = 0.9
BETA_STATS = 0.9
ADAM_EPSILON = 1e-08
CLIP_RMS = 1.0
QUINTIC_A = 3.4445
QUINTIC_B = -4.775
QUINTIC_C = 2.0315
F32, BF16 = jnp.float32, jnp.bfloat16
NN = (((1,), (0,)), ((), ()))
NT = (((1,), (1,)), ((), ()))
BLK = 256


def mxu(a, b, dims=NN):
    return lax.dot_general(a, b, dims, preferred_element_type=F32)


def split(x):
    high = x.astype(BF16)
    return high, (x - high.astype(F32)).astype(BF16)


def store_split(x, high_ref, low_ref, at=slice(None)):
    high, low = split(x)
    high_ref[at, :] = high
    low_ref[at, :] = low


def blocks(ref, n=None):
    n = ref.shape[0]
    return [pl.ds(i, BLK) for i in range(0, n, BLK)]


def prod3(ah, al, bh, bl, at, dims=NN):
    a_high = ah[at, :]
    return mxu(a_high, bh[...], dims) + (mxu(a_high, bl[...], dims) + mxu(al[at, :], bh[...], dims))


def basis_kernel(stats_ref, basis_ref, out_ref, ah, al, bh, bl, xh, xl, gh, gl, y):
    store_split(stats_ref[...], ah, al)
    store_split(basis_ref[...], bh, bl)
    total = jnp.zeros((), F32)
    for at in blocks(stats_ref):
        part = prod3(ah, al, bh, bl, at)
        y[at, :] = part
        total = total + jnp.sum(part * part)
    scale = lax.rsqrt(total + 1e-12)
    y[...] = (y[...] * scale).T
    for _ in range(NS_ITERS):
        store_split(y[...], xh, xl)
        for at in blocks(y):
            store_split(prod3(xh, xl, xh, xl, at, NT), gh, gl, at)
        for at in blocks(y):
            square = prod3(gh, gl, gh, gl, at)
            gram = gh[at, :].astype(F32) + gl[at, :].astype(F32)
            store_split(QUINTIC_B * gram + QUINTIC_C * square, ah, al, at)
        for at in blocks(y):
            y[at, :] = QUINTIC_A * y[at, :] + prod3(ah, al, xh, xl, at)
    out_ref[...] = y[...].T


def basis_call(stats, basis):
    n = stats.shape[0]
    return pl.pallas_call(
        basis_kernel,
        out_shape=jax.ShapeDtypeStruct((n, n), F32),
        in_specs=[pl.BlockSpec(memory_space=pltpu.VMEM)] * 2,
        out_specs=pl.BlockSpec(memory_space=pltpu.VMEM),
        scratch_shapes=[pltpu.VMEM((n, n), BF16)] * 8 + [pltpu.VMEM((n, n), F32)],
        compiler_params=pltpu.CompilerParams(vmem_limit_bytes=24 << 20),
        cost_estimate=pl.CostEstimate(flops=2 * n**3 * 21, bytes_accessed=3 << 20, transcendentals=0),
        name="basis",
    )(stats, basis)


def moment_kernel(left_ref, right_ref, moment_ref, out_ref, lth, ltl, lh, ll, rh, rl, mh, ml):
    left = left_ref[...]
    store_split(left, lh, ll)
    store_split(left.T, lth, ltl)
    store_split(right_ref[...], rh, rl)
    store_split(moment_ref[...], mh, ml)
    for at in blocks(left_ref):
        high, low = split(prod3(lth, ltl, mh, ml, at))
        out_ref[at, :] = mxu(high, rh[...]) + (mxu(high, rl[...]) + mxu(low, rh[...]))


def moment_call(left, right, moment):
    n = left.shape[0]
    half = jax.ShapeDtypeStruct((n, n), BF16)
    return pl.pallas_call(
        moment_kernel,
        out_shape=(jax.ShapeDtypeStruct((n, n), F32),) + (half,) * 6,
        in_specs=[pl.BlockSpec(memory_space=pltpu.VMEM)] * 3,
        out_specs=[pl.BlockSpec(memory_space=pltpu.VMEM)] * 7,
        scratch_shapes=[pltpu.VMEM((n, n), BF16)] * 2,
        compiler_params=pltpu.CompilerParams(vmem_limit_bytes=65_600_000),
        cost_estimate=pl.CostEstimate(flops=2 * n**3 * 6, bytes_accessed=7 << 20, transcendentals=0),
        name="turn",
    )(left, right, moment)


def step_kernel(entries, got_hbm, lth_hbm, ltl_hbm, rh_hbm, rl_hbm, second_hbm, pmq_hbm, lh_hbm, ll_hbm,
                update_hbm, second_out_hbm, factor_ref,
                tile_ref, sums_ref, lth, ltl, rh, rl, second_ref, pmq_ref, lh, ll, dh, dl, update_ref,
                in_sems, out_sems):
    pieces, rows = update_ref.shape[0], update_ref.shape[1]
    n = pieces * rows
    sources = (got_hbm.at[:, pl.ds(0, rows), :], lth_hbm, ltl_hbm, got_hbm.at[:, pl.ds(rows, 8), pl.ds(0, 128)],
               rh_hbm, rl_hbm, second_hbm, pmq_hbm, lh_hbm, ll_hbm)
    targets = (tile_ref, lth, ltl, sums_ref, rh, rl, second_ref, pmq_ref, lh, ll)
    loads = [
        pltpu.make_async_copy(source, target, in_sems.at[i])
        for i, (source, target) in enumerate(zip(sources, targets))
    ]
    for load in loads:
        load.start()
    for load in loads[:3]:
        load.wait()
    tile = tile_ref[...].reshape(n, n)
    for i, at in enumerate(blocks(lth)):
        high, low = split(mxu(lth[at, :], tile) + mxu(ltl[at, :], tile))
        if i == 0:
            for load in loads[3:6]:
                load.wait()
            packed = jnp.sum(sums_ref[...].astype(F32), axis=0)
            energy = packed[0:1, 0:1] + packed[1:2, 0:1] + packed[2:3, 0:1]
            factor = jnp.minimum(1.0, CLIP_RMS / jnp.sqrt(energy / entries + 1e-12))
            factor_ref[...] = jnp.broadcast_to(factor, factor_ref.shape)
        turned = mxu(high, rh[...]) + (mxu(high, rl[...]) + mxu(low, rh[...]))
        if i == 0:
            for load in loads[6:8]:
                load.wait()
        rotated = factor * turned
        second = BETA_SECOND * second_ref[at, :] + (1.0 - BETA_SECOND) * rotated * rotated
        second_ref[at, :] = second
        rotated_moment = BETA_MOMENT * pmq_ref[at, :] + (1.0 - BETA_MOMENT) * rotated
        store_split(rotated_moment / (jnp.sqrt(second) + ADAM_EPSILON), dh, dl, at)
    for load in loads[8:]:
        load.wait()
    count = BLK // rows
    stores = []
    for i, at in enumerate(blocks(lth)):
        high, low = split(prod3(lh, ll, dh, dl, at))
        if i == 0:
            stores.append(pltpu.make_async_copy(second_ref, second_out_hbm, out_sems.at[0]))
            stores[-1].start()
        out = mxu(high, rh[...], NT) + (mxu(high, rl[...], NT) + mxu(low, rh[...], NT))
        if i > 0:
            stores.append(send_rows(update_ref, update_hbm, i - 1, count, out_sems))
        update_ref[i * count : (i + 1) * count] = out.astype(BF16).reshape(count, rows, n)
    stores.append(send_rows(update_ref, update_hbm, n // BLK - 1, count, out_sems))
    for store in stores:
        store.wait()


def send_rows(source, target, i, count, sems):
    part = pl.ds(i * count, count)
    copy = pltpu.make_async_copy(source.at[part], target.at[part], sems.at[i + 1])
    copy.start()
    return copy


def step_call(entries, got, halves, pmq, second):
    n = pmq.shape[0]
    pieces = got.shape[0]
    lth, ltl, lh, ll, rh, rl = halves
    half, full = pltpu.VMEM((n, n), BF16), pltpu.VMEM((n, n), F32)
    hbm = pl.BlockSpec(memory_space=pltpu.HBM)
    vmem = pl.BlockSpec(memory_space=pltpu.VMEM)
    block = pltpu.VMEM((pieces, n // pieces, n), BF16)
    return pl.pallas_call(
        functools.partial(step_kernel, entries),
        out_shape=(
            jax.ShapeDtypeStruct((pieces, n // pieces, n), BF16),
            jax.ShapeDtypeStruct((n, n), F32),
            jax.ShapeDtypeStruct((8, 128), F32),
        ),
        in_specs=[hbm] * 9,
        out_specs=[hbm, hbm, vmem],
        scratch_shapes=[block, pltpu.VMEM((pieces, 8, 128), BF16)]
        + [half] * 4
        + [full] * 2
        + [half] * 4
        + [block, pltpu.SemaphoreType.DMA((10,)), pltpu.SemaphoreType.DMA((n // BLK + 1,))],
        compiler_params=pltpu.CompilerParams(vmem_limit_bytes=66_500_000),
        cost_estimate=pl.CostEstimate(flops=2 * n**3 * 11, bytes_accessed=7 << 20, transcendentals=0),
        name="step",
    )(got, lth, ltl, rh, rl, second, pmq, lh, ll)


def state_kernel(got_ref, factor_ref, moment_ref, left_ref, right_ref, moment_out, left_out, right_out):
    n = moment_ref.shape[0]
    rows = n // got_ref.shape[0]
    tile = got_ref[:, :rows, :].reshape(n, n)
    factor = factor_ref[0:1, 0:1]
    scale = (1.0 - BETA_STATS) * factor * factor / n
    turned = tile.T
    for at in blocks(moment_ref):
        mine = tile[at.start : at.start + BLK, :]
        moment_out[at, :] = BETA_MOMENT * moment_ref[at, :] + (1.0 - BETA_MOMENT) * (factor * mine.astype(F32))
        left_out[at, :] = BETA_STATS * left_ref[at, :] + scale * mxu(mine, tile, NT)
        right_out[at, :] = BETA_STATS * right_ref[at, :] + scale * mxu(turned[at.start : at.start + BLK, :], tile)


def state_call(got, factor, moment, left, right):
    n = moment.shape[0]
    full = jax.ShapeDtypeStruct((n, n), F32)
    return pl.pallas_call(
        state_kernel,
        out_shape=(full,) * 3,
        in_specs=[pl.BlockSpec(memory_space=pltpu.VMEM)] * 5,
        out_specs=[pl.BlockSpec(memory_space=pltpu.VMEM)] * 3,
        compiler_params=pltpu.CompilerParams(vmem_limit_bytes=16 << 20),
        cost_estimate=pl.CostEstimate(flops=2 * n**3 * 2, bytes_accessed=7 << 20, transcendentals=0),
        name="state",
    )(got, factor, moment, left, right)


def energy_kernel(grads_ref, out_ref):
    x = grads_ref[...].astype(F32)
    out_ref[...] = jnp.full(out_ref.shape, jnp.sum(x * x))


def energy_call(grads):
    return pl.pallas_call(
        energy_kernel,
        out_shape=jax.ShapeDtypeStruct((8, 128), F32),
        in_specs=[pl.BlockSpec(memory_space=pltpu.VMEM)],
        out_specs=pl.BlockSpec(memory_space=pltpu.VMEM),
        compiler_params=pltpu.CompilerParams(vmem_limit_bytes=4 << 20),
        cost_estimate=pl.CostEstimate(flops=1 << 19, bytes_accessed=1 << 19, transcendentals=0),
        name="energy",
    )(grads)


def route_kernel(slots_ref, own_ref, other_ref, energy_ref, out_ref, source_ref):
    chips, rows = own_ref.shape[0], own_ref.shape[1]
    core = lax.rem(lax.axis_index("shard"), 2)
    for i in range(2 * chips):
        source_ref[slots_ref[0, i]] = i
    energy = energy_ref[...]
    high = energy.astype(BF16).astype(F32)
    middle = (energy - high).astype(BF16).astype(F32)
    low = energy - high - middle
    row = lax.broadcasted_iota(jnp.int32, energy.shape, 0)
    packed = jnp.where(row == 0, high, jnp.where(row == 1, middle, low)).astype(BF16)
    packed = jnp.concatenate([packed] * (out_ref.shape[2] // 128), axis=1)
    for chip in range(chips):
        block = source_ref[2 * chip + core]
        mine = lax.rem(block, 2) == core
        out_ref[chip, :rows, :] = jnp.where(mine, own_ref[block // 2], other_ref[block // 2])
        out_ref[chip, rows:, :] = packed


def return_kernel(slots_ref, own_ref, other_ref, out_ref):
    core = lax.rem(lax.axis_index("shard"), 2)
    for i in range(own_ref.shape[0]):
        slot = slots_ref[0, 2 * i + core]
        mine = lax.rem(slot, 2) == core
        out_ref[i] = jnp.where(mine, own_ref[slot // 2], other_ref[slot // 2])


def pick_call(kernel, rows, scratch, operands):
    chips, size = operands[1].shape[0], operands[1].shape[2]
    return pl.pallas_call(
        kernel,
        out_shape=jax.ShapeDtypeStruct((chips, rows, size), BF16),
        in_specs=[pl.BlockSpec(memory_space=pltpu.SMEM)]
        + [pl.BlockSpec(memory_space=pltpu.VMEM)] * (len(operands) - 1),
        out_specs=pl.BlockSpec(memory_space=pltpu.VMEM),
        scratch_shapes=scratch,
        compiler_params=pltpu.CompilerParams(vmem_limit_bytes=8 << 20),
        cost_estimate=pl.CostEstimate(flops=0, bytes_accessed=1 << 21, transcendentals=0),
    )(*operands)


def shards(grads, assignment, moment, second, left_stats, right_stats, left_basis, right_basis):
    shard_count = lax.axis_size("shard")
    tensor_count = lax.axis_size("tensor")
    size = grads.shape[1]
    chips = shard_count // 2
    rows = size // chips
    entries = float(size * size * shard_count * tensor_count)
    same_core = [[2 * p + q for p in range(chips)] for q in range(2)]
    swap = [(i, i ^ 1) for i in range(shard_count)]
    moment, second = moment[0], second[0]
    left_stats, right_stats = left_stats[0], right_stats[0]
    left_basis, right_basis = left_basis[0], right_basis[0]

    def exchange(pieces):
        return lax.all_to_all(pieces, "shard", 0, 0, axis_index_groups=same_core)

    arrived = exchange(grads.reshape(chips, rows, size))
    energy = energy_call(grads)
    moved = [
        lax.ppermute(
            energy, "tensor", [(i, (i + s) % tensor_count) for i in range(tensor_count)]
        )
        for s in range(1, tensor_count)
    ]
    turned, *halves = moment_call(left_basis, right_basis, moment)
    moved, turned = lax.optimization_barrier((moved, turned))
    for part in moved:
        energy = energy + part
    energy = energy + lax.ppermute(energy, "shard", swap)
    other = lax.ppermute(arrived, "shard", swap)
    routed = pick_call(
        route_kernel, rows + 8, [pltpu.SMEM((shard_count,), jnp.int32)], (assignment, arrived, other, energy)
    )
    got = exchange(routed)
    left_basis_new = basis_call(left_stats, left_basis)
    update, second_new, factor = step_call(entries, got, halves, turned, second)
    returned = exchange(update)
    right_basis_new = basis_call(right_stats, right_basis)
    other = lax.ppermute(returned, "shard", swap)
    picked = pick_call(return_kernel, rows, [], (assignment, returned, other))
    update_out = exchange(picked).reshape(size, size)
    moment_new, left_new, right_new = state_call(got, factor, moment, left_stats, right_stats)

    states = (moment_new, second_new, left_new, right_new, left_basis_new, right_basis_new)
    return (update_out,) + tuple(state[None] for state in states)


def solution(mesh):
    weights = P("shard", "tensor")
    state = P("shard", "tensor", None)

    return jax.shard_map(
        shards,
        mesh=mesh,
        in_specs=(weights, P("tensor", None)) + (state,) * 6,
        out_specs=(weights,) + (state,) * 6,
        check_vma=False,
    )
```

```python
import functools
import jax
import jax.numpy as jnp
from jax import lax
from jax.experimental import pallas as pl
from jax.experimental.pallas import tpu as pltpu
from jax.sharding import PartitionSpec as P


NS_ITERS = 2
BETA_MOMENT = 0.9
BETA_SECOND = 0.9
BETA_STATS = 0.9
ADAM_EPSILON = 1e-08
CLIP_RMS = 1.0
QUINTIC_A = 3.4445
QUINTIC_B = -4.775
QUINTIC_C = 2.0315
F32, BF16 = jnp.float32, jnp.bfloat16
NN = (((1,), (0,)), ((), ()))
NT = (((1,), (1,)), ((), ()))
BLK = 256


def mxu(a, b, dims=NN):
    return lax.dot_general(a, b, dims, preferred_element_type=F32)


def split(x):
    high = x.astype(BF16)
    return high, (x - high.astype(F32)).astype(BF16)


def store_split(x, high_ref, low_ref, at=slice(None)):
    high, low = split(x)
    high_ref[at, :] = high
    low_ref[at, :] = low


def blocks(ref, n=None):
    n = ref.shape[0]
    return [pl.ds(i, BLK) for i in range(0, n, BLK)]


def prod3(ah, al, bh, bl, at, dims=NN):
    a_high = ah[at, :]
    return mxu(a_high, bh[...], dims) + (mxu(a_high, bl[...], dims) + mxu(al[at, :], bh[...], dims))


def sweep(y, ah, al, xh, xl, gh, gl):
    store_split(y[...], xh, xl)
    for at in blocks(y):
        store_split(prod3(xh, xl, xh, xl, at, NT), gh, gl, at)
    for at in blocks(y):
        square = prod3(gh, gl, gh, gl, at)
        gram = gh[at, :].astype(F32) + gl[at, :].astype(F32)
        store_split(QUINTIC_B * gram + QUINTIC_C * square, ah, al, at)
    for at in blocks(y):
        y[at, :] = QUINTIC_A * y[at, :] + prod3(ah, al, xh, xl, at)


def open_kernel(sweeps, stats_ref, basis_ref, y, ah, al, xh, xl, gh, gl):
    store_split(stats_ref[...], ah, al)
    store_split(basis_ref[...], xh, xl)
    total = jnp.zeros((), F32)
    for at in blocks(stats_ref):
        part = prod3(ah, al, xh, xl, at)
        y[at, :] = part
        total = total + jnp.sum(part * part)
    scale = lax.rsqrt(total + 1e-12)
    y[...] = (y[...] * scale).T
    for _ in range(sweeps):
        sweep(y, ah, al, xh, xl, gh, gl)
    if sweeps == NS_ITERS:
        y[...] = y[...].T


def close_kernel(sweeps, start_ref, out_ref, y, ah, al, xh, xl, gh, gl):
    y[...] = start_ref[...]
    for _ in range(sweeps):
        sweep(y, ah, al, xh, xl, gh, gl)
    out_ref[...] = y[...].T


def basis_call(kernel, sweeps, operands, extra):
    n = operands[0].shape[0]
    return pl.pallas_call(
        functools.partial(kernel, sweeps),
        out_shape=jax.ShapeDtypeStruct((n, n), F32),
        in_specs=[pl.BlockSpec(memory_space=pltpu.VMEM)] * len(operands),
        out_specs=pl.BlockSpec(memory_space=pltpu.VMEM),
        scratch_shapes=[pltpu.VMEM((n, n), F32)] * extra + [pltpu.VMEM((n, n), BF16)] * 6,
        compiler_params=pltpu.CompilerParams(vmem_limit_bytes=64_900_000),
        cost_estimate=pl.CostEstimate(flops=2 * n**3 * 9 * sweeps, bytes_accessed=3 << 20, transcendentals=0),
    )(*operands)


def open_basis(stats, basis, sweeps):
    return basis_call(open_kernel, sweeps, (stats, basis), 0)


def close_basis(start, sweeps):
    return basis_call(close_kernel, sweeps, (start,), 1)


def moment_kernel(left_ref, right_ref, moment_ref, out_ref, lth, ltl, lh, ll, rh, rl, mh, ml):
    left = left_ref[...]
    store_split(left, lh, ll)
    store_split(left.T, lth, ltl)
    store_split(right_ref[...], rh, rl)
    store_split(moment_ref[...], mh, ml)
    for at in blocks(left_ref):
        high, low = split(prod3(lth, ltl, mh, ml, at))
        out_ref[at, :] = mxu(high, rh[...]) + (mxu(high, rl[...]) + mxu(low, rh[...]))


def moment_call(left, right, moment):
    n = left.shape[0]
    half = jax.ShapeDtypeStruct((n, n), BF16)
    return pl.pallas_call(
        moment_kernel,
        out_shape=(jax.ShapeDtypeStruct((n, n), F32),) + (half,) * 6,
        in_specs=[pl.BlockSpec(memory_space=pltpu.VMEM)] * 3,
        out_specs=[pl.BlockSpec(memory_space=pltpu.VMEM)] * 7,
        scratch_shapes=[pltpu.VMEM((n, n), BF16)] * 2,
        compiler_params=pltpu.CompilerParams(vmem_limit_bytes=65_600_000),
        cost_estimate=pl.CostEstimate(flops=2 * n**3 * 6, bytes_accessed=7 << 20, transcendentals=0),
        name="turn",
    )(left, right, moment)


def tiles(rows, n):
    across = n // 128
    return [
        (pl.ds((high * across + wide) * 16, 16), pl.ds(high * 16, 16), pl.ds(wide * 128, 128))
        for high in range(rows // 16)
        for wide in range(across)
    ]


def step_kernel(entries, got_hbm, lth_hbm, ltl_hbm, rh_hbm, rl_hbm, second_hbm, pmq_hbm, lh_hbm, ll_hbm,
                update_hbm, second_out_hbm, factor_ref,
                got_ref, tile_ref, lth, ltl, rh, rl, second_ref, pmq_ref, lh, ll, dh, dl, update_ref,
                in_sems, out_sems):
    pieces, rows = update_ref.shape[0], update_ref.shape[1]
    n = pieces * rows
    pairs = [(got_hbm, got_ref), (lth_hbm, lth), (ltl_hbm, ltl)]
    pairs += [(rh_hbm, rh), (rl_hbm, rl), (second_hbm, second_ref), (pmq_hbm, pmq_ref), (lh_hbm, lh), (ll_hbm, ll)]
    loads = [pltpu.make_async_copy(source, target, in_sems.at[i]) for i, (source, target) in enumerate(pairs)]
    for load in loads:
        load.start()
    loads[0].wait()
    for part, high, wide in tiles(rows, n):
        tile_ref[:, high, wide] = got_ref[:, part, :]
    for load in loads[1:3]:
        load.wait()
    packed = jnp.sum(got_ref[:, rows * n // 128 :, :].astype(F32), axis=0)
    energy = packed[0:1, 0:1] + packed[1:2, 0:1] + packed[2:3, 0:1]
    factor = jnp.minimum(1.0, CLIP_RMS / jnp.sqrt(energy / entries + 1e-12))
    factor_ref[...] = jnp.broadcast_to(factor, factor_ref.shape)
    tile = tile_ref[...].reshape(n, n)
    for i, at in enumerate(blocks(lth)):
        high, low = split(mxu(lth[at, :], tile) + mxu(ltl[at, :], tile))
        if i == 0:
            for load in loads[3:5]:
                load.wait()
        turned = mxu(high, rh[...]) + (mxu(high, rl[...]) + mxu(low, rh[...]))
        if i == 0:
            for load in loads[5:7]:
                load.wait()
        rotated = factor * turned
        second = BETA_SECOND * second_ref[at, :] + (1.0 - BETA_SECOND) * rotated * rotated
        second_ref[at, :] = second
        rotated_moment = BETA_MOMENT * pmq_ref[at, :] + (1.0 - BETA_MOMENT) * rotated
        store_split(rotated_moment / (jnp.sqrt(second) + ADAM_EPSILON), dh, dl, at)
    for load in loads[7:]:
        load.wait()
    count = BLK // rows
    stores = []
    for i, at in enumerate(blocks(lth)):
        high, low = split(prod3(lh, ll, dh, dl, at))
        if i == 0:
            stores.append(pltpu.make_async_copy(second_ref, second_out_hbm, out_sems.at[0]))
            stores[-1].start()
        out = mxu(high, rh[...], NT) + (mxu(high, rl[...], NT) + mxu(low, rh[...], NT))
        if i > 0:
            stores.append(send_rows(update_ref, update_hbm, i - 1, count, out_sems))
        update_ref[i * count : (i + 1) * count] = out.astype(BF16).reshape(count, rows, n)
    stores.append(send_rows(update_ref, update_hbm, n // BLK - 1, count, out_sems))
    for store in stores:
        store.wait()


def send_rows(source, target, i, count, sems):
    part = pl.ds(i * count, count)
    copy = pltpu.make_async_copy(source.at[part], target.at[part], sems.at[i + 1])
    copy.start()
    return copy


def step_call(entries, got, halves, pmq, second):
    n = pmq.shape[0]
    pieces = got.shape[0]
    lth, ltl, lh, ll, rh, rl = halves
    half, full = pltpu.VMEM((n, n), BF16), pltpu.VMEM((n, n), F32)
    hbm = pl.BlockSpec(memory_space=pltpu.HBM)
    vmem = pl.BlockSpec(memory_space=pltpu.VMEM)
    block = pltpu.VMEM((pieces, n // pieces, n), BF16)
    return pl.pallas_call(
        functools.partial(step_kernel, entries),
        out_shape=(
            jax.ShapeDtypeStruct((pieces, n // pieces, n), BF16),
            jax.ShapeDtypeStruct((n, n), F32),
            jax.ShapeDtypeStruct((8, 128), F32),
        ),
        in_specs=[hbm] * 9,
        out_specs=[hbm, hbm, vmem],
        scratch_shapes=[pltpu.VMEM(got.shape, BF16), block]
        + [half] * 4
        + [full] * 2
        + [half] * 4
        + [block, pltpu.SemaphoreType.DMA((9,)), pltpu.SemaphoreType.DMA((n // BLK + 1,))],
        compiler_params=pltpu.CompilerParams(vmem_limit_bytes=66_500_000),
        cost_estimate=pl.CostEstimate(flops=2 * n**3 * 11, bytes_accessed=7 << 20, transcendentals=0),
        name="step",
    )(got, lth, ltl, rh, rl, second, pmq, lh, ll)


def state_kernel(got_ref, factor_ref, moment_ref, left_ref, right_ref, moment_out, left_out, right_out, tile_ref):
    n = moment_ref.shape[0]
    rows = tile_ref.shape[1]
    for part, high, wide in tiles(rows, n):
        tile_ref[:, high, wide] = got_ref[:, part, :]
    tile = tile_ref[...].reshape(n, n)
    factor = factor_ref[0:1, 0:1]
    scale = (1.0 - BETA_STATS) * factor * factor / n
    turned = tile.T
    for at in blocks(moment_ref):
        mine = tile[at.start : at.start + BLK, :]
        moment_out[at, :] = BETA_MOMENT * moment_ref[at, :] + (1.0 - BETA_MOMENT) * (factor * mine.astype(F32))
        left_out[at, :] = BETA_STATS * left_ref[at, :] + scale * mxu(mine, tile, NT)
        right_out[at, :] = BETA_STATS * right_ref[at, :] + scale * mxu(turned[at.start : at.start + BLK, :], tile)


def state_call(got, factor, moment, left, right):
    n = moment.shape[0]
    full = jax.ShapeDtypeStruct((n, n), F32)
    return pl.pallas_call(
        state_kernel,
        out_shape=(full,) * 3,
        in_specs=[pl.BlockSpec(memory_space=pltpu.VMEM)] * 5,
        out_specs=[pl.BlockSpec(memory_space=pltpu.VMEM)] * 3,
        scratch_shapes=[pltpu.VMEM((got.shape[0], n // got.shape[0], n), BF16)],
        compiler_params=pltpu.CompilerParams(vmem_limit_bytes=66_500_000),
        cost_estimate=pl.CostEstimate(flops=2 * n**3 * 2, bytes_accessed=7 << 20, transcendentals=0),
        name="state",
    )(got, factor, moment, left, right)


def energy_kernel(grads_ref, out_ref):
    x = grads_ref[...].astype(F32)
    out_ref[...] = jnp.full(out_ref.shape, jnp.sum(x * x))


def energy_call(grads):
    return pl.pallas_call(
        energy_kernel,
        out_shape=jax.ShapeDtypeStruct((8, 128), F32),
        in_specs=[pl.BlockSpec(memory_space=pltpu.VMEM)],
        out_specs=pl.BlockSpec(memory_space=pltpu.VMEM),
        compiler_params=pltpu.CompilerParams(vmem_limit_bytes=4 << 20),
        cost_estimate=pl.CostEstimate(flops=1 << 19, bytes_accessed=1 << 19, transcendentals=0),
        name="energy",
    )(grads)


def route_kernel(slots_ref, own_ref, other_ref, energy_ref, out_ref, source_ref):
    chips, rows = own_ref.shape[0], own_ref.shape[1]
    core = lax.rem(lax.axis_index("shard"), 2)
    for i in range(2 * chips):
        source_ref[slots_ref[0, i]] = i
    energy = energy_ref[...]
    high = energy.astype(BF16).astype(F32)
    middle = (energy - high).astype(BF16).astype(F32)
    low = energy - high - middle
    row = lax.broadcasted_iota(jnp.int32, energy.shape, 0)
    packed = jnp.where(row == 0, high, jnp.where(row == 1, middle, low)).astype(BF16)
    for chip in range(chips):
        block = source_ref[2 * chip + core]
        mine = lax.rem(block, 2) == core
        for part, high, wide in tiles(rows, own_ref.shape[2]):
            out_ref[chip, part, :] = jnp.where(mine, own_ref[block // 2, high, wide], other_ref[block // 2, high, wide])
        out_ref[chip, out_ref.shape[1] - 8 :, :] = packed


def return_kernel(slots_ref, own_ref, other_ref, out_ref):
    core = lax.rem(lax.axis_index("shard"), 2)
    for i in range(own_ref.shape[0]):
        slot = slots_ref[0, 2 * i + core]
        mine = lax.rem(slot, 2) == core
        out_ref[i] = jnp.where(mine, own_ref[slot // 2], other_ref[slot // 2])


def pick_call(kernel, shape, scratch, operands):
    return pl.pallas_call(
        kernel,
        out_shape=jax.ShapeDtypeStruct(shape, BF16),
        in_specs=[pl.BlockSpec(memory_space=pltpu.SMEM)]
        + [pl.BlockSpec(memory_space=pltpu.VMEM)] * (len(operands) - 1),
        out_specs=pl.BlockSpec(memory_space=pltpu.VMEM),
        scratch_shapes=scratch,
        compiler_params=pltpu.CompilerParams(vmem_limit_bytes=8 << 20),
        cost_estimate=pl.CostEstimate(flops=0, bytes_accessed=1 << 21, transcendentals=0),
    )(*operands)


def shards(grads, assignment, moment, second, left_stats, right_stats, left_basis, right_basis):
    shard_count = lax.axis_size("shard")
    tensor_count = lax.axis_size("tensor")
    size = grads.shape[1]
    chips = shard_count // 2
    rows = size // chips
    entries = float(size * size * shard_count * tensor_count)
    same_core = [[2 * p + q for p in range(chips)] for q in range(2)]
    swap = [(i, i ^ 1) for i in range(shard_count)]
    moment, second = moment[0], second[0]
    left_stats, right_stats = left_stats[0], right_stats[0]
    left_basis, right_basis = left_basis[0], right_basis[0]

    def exchange(pieces):
        return lax.all_to_all(pieces, "shard", 0, 0, axis_index_groups=same_core)

    arrived = exchange(grads.reshape(chips, rows, size))
    energy = energy_call(grads)
    moved = [
        lax.ppermute(
            energy, "tensor", [(i, (i + s) % tensor_count) for i in range(tensor_count)]
        )
        for s in range(1, tensor_count)
    ]
    for part in moved:
        energy = energy + part
    energy = energy + lax.ppermute(energy, "shard", swap)
    other = lax.ppermute(arrived, "shard", swap)
    routed = pick_call(
        route_kernel,
        (chips, rows * size // 128 + 8, 128),
        [pltpu.SMEM((shard_count,), jnp.int32)],
        (assignment, arrived, other, energy),
    )
    got = exchange(routed)
    turned, *halves = moment_call(left_basis, right_basis, moment)
    left_half = open_basis(left_stats, left_basis, 1)
    update, second_new, factor = step_call(entries, got, halves, turned, second)
    returned = exchange(update)
    right_basis_new = open_basis(right_stats, right_basis, NS_ITERS)
    other = lax.ppermute(returned, "shard", swap)
    picked = pick_call(return_kernel, (chips, rows, size), [], (assignment, returned, other))
    update_out = exchange(picked).reshape(size, size)
    left_basis_new = close_basis(left_half, NS_ITERS - 1)
    moment_new, left_new, right_new = state_call(got, factor, moment, left_stats, right_stats)

    states = (moment_new, second_new, left_new, right_new, left_basis_new, right_basis_new)
    return (update_out,) + tuple(state[None] for state in states)


def solution(mesh):
    weights = P("shard", "tensor")
    state = P("shard", "tensor", None)

    return jax.shard_map(
        shards,
        mesh=mesh,
        in_specs=(weights, P("tensor", None)) + (state,) * 6,
        out_specs=(weights,) + (state,) * 6,
        check_vma=False,
    )
```

```python
import functools
import jax
import jax.numpy as jnp
from jax import lax
from jax.experimental import pallas as pl
from jax.experimental.pallas import tpu as pltpu
from jax.sharding import PartitionSpec as P


NS_ITERS = 2
BETA_MOMENT = 0.9
BETA_SECOND = 0.9
BETA_STATS = 0.9
ADAM_EPSILON = 1e-08
CLIP_RMS = 1.0
QUINTIC_A = 3.4445
QUINTIC_B = -4.775
QUINTIC_C = 2.0315
F32, BF16 = jnp.float32, jnp.bfloat16
NN = (((1,), (0,)), ((), ()))
NT = (((1,), (1,)), ((), ()))
BLK = 256


def mxu(a, b, dims=NN):
    return lax.dot_general(a, b, dims, preferred_element_type=F32)


def split(x):
    high = x.astype(BF16)
    return high, (x - high.astype(F32)).astype(BF16)


def store_split(x, high_ref, low_ref, at=slice(None)):
    high, low = split(x)
    high_ref[at, :] = high
    low_ref[at, :] = low


def blocks(ref, n=None):
    n = ref.shape[0]
    return [pl.ds(i, BLK) for i in range(0, n, BLK)]


def prod3(ah, al, bh, bl, at, dims=NN):
    a_high = ah[at, :]
    return mxu(a_high, bh[...], dims) + (mxu(a_high, bl[...], dims) + mxu(al[at, :], bh[...], dims))


def polynomial(y, ah, al, xh, xl, gh, gl):
    store_split(y[...], xh, xl)
    for at in blocks(y):
        store_split(prod3(xh, xl, xh, xl, at, NT), gh, gl, at)
    for at in blocks(y):
        square = prod3(gh, gl, gh, gl, at)
        gram = gh[at, :].astype(F32) + gl[at, :].astype(F32)
        store_split(QUINTIC_B * gram + QUINTIC_C * square, ah, al, at)


def sweep(y, ah, al, xh, xl, gh, gl):
    polynomial(y, ah, al, xh, xl, gh, gl)
    for at in blocks(y):
        y[at, :] = QUINTIC_A * y[at, :] + prod3(ah, al, xh, xl, at)


def last_sweep(y, ah, al, xh, xl, gh, gl, out, out_hbm, stores):
    polynomial(y, ah, al, xh, xl, gh, gl)
    gh[...] = xh[...].T
    gl[...] = xl[...].T
    before = None
    for at in blocks(y):
        rows = gh[at, :].astype(F32) + gl[at, :].astype(F32)
        out[at, :] = QUINTIC_A * rows + prod3(gh, gl, ah, al, at)
        if before is not None:
            stores.add(out.at[before, :], out_hbm.at[before, :])
        before = at
    stores.add(out.at[before, :], out_hbm.at[before, :])


def make_loads(pairs, sems):
    return [pltpu.make_async_copy(source, target, sems.at[i]) for i, (source, target) in enumerate(pairs)]


class Stores:
    def __init__(self, sems):
        self.sems, self.copies = sems, []

    def add(self, source, target):
        copy = pltpu.make_async_copy(source, target, self.sems.at[len(self.copies)])
        copy.start()
        self.copies.append(copy)

    def wait(self):
        for copy in self.copies:
            copy.wait()


def first_iterate(y, ah, al, bth, btl):
    total = jnp.zeros((), F32)
    for at in blocks(y):
        part = prod3(bth, btl, ah, al, at, NT)
        y[at, :] = part
        total = total + jnp.sum(part * part)
    y[...] = y[...] * lax.rsqrt(total + 1e-12)


def early_kernel(left_hbm, stats_hbm, right_hbm, moment_hbm,
                 y_hbm, pmq_hbm, lth_hbm, ltl_hbm, lh_hbm, ll_hbm, rh_hbm, rl_hbm,
                 left, stats, right, moment, y, pmq, lth, ltl, lh, ll, rh, rl, ah, al, xh, xl, gh, gl,
                 in_sems, out_sems):
    pairs = ((left_hbm, left), (stats_hbm, stats), (right_hbm, right), (moment_hbm, moment))
    loads = make_loads(pairs, in_sems)
    stores = Stores(out_sems)
    loads[0].start()
    loads[1].start()
    loads[0].wait()
    store_split(left[...].T, lth, ltl)
    loads[1].wait()
    loads[2].start()
    loads[3].start()
    store_split(stats[...], ah, al)
    first_iterate(y, ah, al, lth, ltl)
    store_split(left[...], lh, ll)
    for source, target in ((lth, lth_hbm), (ltl, ltl_hbm), (lh, lh_hbm), (ll, ll_hbm)):
        stores.add(source, target)
    sweep(y, ah, al, xh, xl, gh, gl)
    loads[2].wait()
    store_split(right[...], rh, rl)
    stores.add(y, y_hbm)
    loads[3].wait()
    store_split(moment[...], xh, xl)
    stores.add(rh, rh_hbm)
    stores.add(rl, rl_hbm)
    before = None
    for at in blocks(pmq):
        high, low = split(prod3(lth, ltl, xh, xl, at))
        if before is not None:
            stores.add(pmq.at[before, :], pmq_hbm.at[before, :])
        pmq[at, :] = mxu(high, rh[...]) + (mxu(high, rl[...]) + mxu(low, rh[...]))
        before = at
    stores.add(pmq.at[before, :], pmq_hbm.at[before, :])
    stores.wait()


def right_kernel(stats_hbm, basis_hbm, out_hbm, stats, basis, y, ah, al, xh, xl, gh, gl, in_sems, out_sems):
    loads = make_loads(((basis_hbm, basis), (stats_hbm, stats)), in_sems)
    stores = Stores(out_sems)
    for load in loads:
        load.start()
    loads[0].wait()
    store_split(basis[...].T, xh, xl)
    loads[1].wait()
    store_split(stats[...], ah, al)
    first_iterate(y, ah, al, xh, xl)
    for _ in range(NS_ITERS - 1):
        sweep(y, ah, al, xh, xl, gh, gl)
    last_sweep(y, ah, al, xh, xl, gh, gl, stats, out_hbm, stores)
    stores.wait()


def late_kernel(y_hbm, got_hbm, factor_hbm, moment_hbm, left_hbm, right_hbm,
                basis_hbm, moment_out, left_out, right_out,
                y, got, factor_ref, moment, left, right, tile_ref, turned, out, ah, al, xh, xl, gh, gl,
                in_sems, out_sems):
    n, rows = moment.shape[0], tile_ref.shape[1]
    pairs = ((y_hbm, y), (got_hbm, got), (factor_hbm, factor_ref))
    pairs += ((moment_hbm, moment), (left_hbm, left), (right_hbm, right))
    loads = make_loads(pairs, in_sems)
    stores = Stores(out_sems)
    loads[0].start()
    loads[0].wait()
    for load in loads[1:]:
        load.start()
    last_sweep(y, ah, al, xh, xl, gh, gl, out, basis_hbm, stores)
    for load in loads[1:]:
        load.wait()
    for part, high, wide in tiles(rows, n):
        tile_ref[:, high, wide] = got[:, part, :]
    tile = tile_ref[...].reshape(n, n)
    turned[...] = tile.T
    factor = factor_ref[0:1, 0:1]
    scale = (1.0 - BETA_STATS) * factor * factor / n
    before = None
    for at in blocks(moment):
        mine = tile[at.start : at.start + BLK, :]
        moment[at, :] = BETA_MOMENT * moment[at, :] + (1.0 - BETA_MOMENT) * (factor * mine.astype(F32))
        left[at, :] = BETA_STATS * left[at, :] + scale * mxu(mine, tile, NT)
        right[at, :] = BETA_STATS * right[at, :] + scale * mxu(turned[at, :], tile)
        for part in (before, at if at.start + BLK == n else None):
            if part is not None:
                for source, target in ((moment, moment_out), (left, left_out), (right, right_out)):
                    stores.add(source.at[part, :], target.at[part, :])
        before = at
    stores.wait()


def window_call(kernel, operands, outs, scratch, passes, limit):
    hbm = pl.BlockSpec(memory_space=pltpu.HBM)
    n = outs[0].shape[0]
    return pl.pallas_call(
        kernel,
        out_shape=outs,
        in_specs=[hbm] * len(operands),
        out_specs=[hbm] * len(outs),
        scratch_shapes=scratch + [pltpu.SemaphoreType.DMA((8,)), pltpu.SemaphoreType.DMA((12,))],
        compiler_params=pltpu.CompilerParams(vmem_limit_bytes=limit),
        cost_estimate=pl.CostEstimate(flops=2 * n**3 * passes, bytes_accessed=8 << 20, transcendentals=0),
    )(*operands)


def early_call(left, stats, right, moment):
    n = left.shape[0]
    full, half = (n, n), pltpu.VMEM((n, n), BF16)
    outs = (jax.ShapeDtypeStruct(full, F32),) * 2 + (jax.ShapeDtypeStruct(full, BF16),) * 6
    scratch = [pltpu.VMEM(full, F32)] * 6 + [half] * 12
    return window_call(early_kernel, (left, stats, right, moment), outs, scratch, 18, 65_600_000)


def right_call(stats, basis):
    n = stats.shape[0]
    scratch = [pltpu.VMEM((n, n), F32)] * 3 + [pltpu.VMEM((n, n), BF16)] * 6
    outs = (jax.ShapeDtypeStruct((n, n), F32),)
    return window_call(right_kernel, (stats, basis), outs, scratch, 21, 65_600_000)[0]


def late_call(half, got, factor, moment, left, right):
    n = half.shape[0]
    full = pltpu.VMEM((n, n), F32)
    scratch = [full, pltpu.VMEM(got.shape, BF16), pltpu.VMEM(factor.shape, F32)] + [full] * 3
    scratch += [pltpu.VMEM((got.shape[0], n // got.shape[0], n), BF16), pltpu.VMEM((n, n), BF16), full]
    scratch += [pltpu.VMEM((n, n), BF16)] * 6
    outs = (jax.ShapeDtypeStruct((n, n), F32),) * 4
    return window_call(late_kernel, (half, got, factor, moment, left, right), outs, scratch, 11, 65_600_000)


def tiles(rows, n):
    across = n // 128
    return [
        (pl.ds((high * across + wide) * 16, 16), pl.ds(high * 16, 16), pl.ds(wide * 128, 128))
        for high in range(rows // 16)
        for wide in range(across)
    ]


def step_kernel(entries, got_hbm, lth_hbm, ltl_hbm, rh_hbm, rl_hbm, second_hbm, pmq_hbm, lh_hbm, ll_hbm,
                update_hbm, second_out_hbm, factor_ref,
                got_ref, tile_ref, lth, ltl, rh, rl, second_ref, pmq_ref, lh, ll, dh, dl, update_ref,
                in_sems, out_sems):
    pieces, rows = update_ref.shape[0], update_ref.shape[1]
    n = pieces * rows
    pairs = [(got_hbm, got_ref), (lth_hbm, lth), (ltl_hbm, ltl)]
    pairs += [(rh_hbm, rh), (rl_hbm, rl), (second_hbm, second_ref), (pmq_hbm, pmq_ref), (lh_hbm, lh), (ll_hbm, ll)]
    loads = [pltpu.make_async_copy(source, target, in_sems.at[i]) for i, (source, target) in enumerate(pairs)]
    for load in loads:
        load.start()
    loads[0].wait()
    for part, high, wide in tiles(rows, n):
        tile_ref[:, high, wide] = got_ref[:, part, :]
    for load in loads[1:3]:
        load.wait()
    packed = jnp.sum(got_ref[:, rows * n // 128 :, :].astype(F32), axis=0)
    energy = packed[0:1, 0:1] + packed[1:2, 0:1] + packed[2:3, 0:1]
    factor = jnp.minimum(1.0, CLIP_RMS / jnp.sqrt(energy / entries + 1e-12))
    factor_ref[...] = jnp.broadcast_to(factor, factor_ref.shape)
    tile = tile_ref[...].reshape(n, n)
    for i, at in enumerate(blocks(lth)):
        high, low = split(mxu(lth[at, :], tile) + mxu(ltl[at, :], tile))
        if i == 0:
            for load in loads[3:5]:
                load.wait()
        turned = mxu(high, rh[...]) + (mxu(high, rl[...]) + mxu(low, rh[...]))
        if i == 0:
            for load in loads[5:7]:
                load.wait()
        rotated = factor * turned
        second = BETA_SECOND * second_ref[at, :] + (1.0 - BETA_SECOND) * rotated * rotated
        second_ref[at, :] = second
        rotated_moment = BETA_MOMENT * pmq_ref[at, :] + (1.0 - BETA_MOMENT) * rotated
        store_split(rotated_moment / (jnp.sqrt(second) + ADAM_EPSILON), dh, dl, at)
    for load in loads[7:]:
        load.wait()
    count = BLK // rows
    stores = []
    for i, at in enumerate(blocks(lth)):
        high, low = split(prod3(lh, ll, dh, dl, at))
        if i == 0:
            stores.append(pltpu.make_async_copy(second_ref, second_out_hbm, out_sems.at[0]))
            stores[-1].start()
        out = mxu(high, rh[...], NT) + (mxu(high, rl[...], NT) + mxu(low, rh[...], NT))
        if i > 0:
            stores.append(send_rows(update_ref, update_hbm, i - 1, count, out_sems))
        update_ref[i * count : (i + 1) * count] = out.astype(BF16).reshape(count, rows, n)
    stores.append(send_rows(update_ref, update_hbm, n // BLK - 1, count, out_sems))
    for store in stores:
        store.wait()


def send_rows(source, target, i, count, sems):
    part = pl.ds(i * count, count)
    copy = pltpu.make_async_copy(source.at[part], target.at[part], sems.at[i + 1])
    copy.start()
    return copy


def step_call(entries, got, halves, pmq, second):
    n = pmq.shape[0]
    pieces = got.shape[0]
    lth, ltl, lh, ll, rh, rl = halves
    half, full = pltpu.VMEM((n, n), BF16), pltpu.VMEM((n, n), F32)
    hbm = pl.BlockSpec(memory_space=pltpu.HBM)
    vmem = pl.BlockSpec(memory_space=pltpu.VMEM)
    block = pltpu.VMEM((pieces, n // pieces, n), BF16)
    return pl.pallas_call(
        functools.partial(step_kernel, entries),
        out_shape=(
            jax.ShapeDtypeStruct((pieces, n // pieces, n), BF16),
            jax.ShapeDtypeStruct((n, n), F32),
            jax.ShapeDtypeStruct((8, 128), F32),
        ),
        in_specs=[hbm] * 9,
        out_specs=[hbm, hbm, vmem],
        scratch_shapes=[pltpu.VMEM(got.shape, BF16), block]
        + [half] * 4
        + [full] * 2
        + [half] * 4
        + [block, pltpu.SemaphoreType.DMA((9,)), pltpu.SemaphoreType.DMA((n // BLK + 1,))],
        compiler_params=pltpu.CompilerParams(vmem_limit_bytes=66_500_000),
        cost_estimate=pl.CostEstimate(flops=2 * n**3 * 11, bytes_accessed=7 << 20, transcendentals=0),
        name="step",
    )(got, lth, ltl, rh, rl, second, pmq, lh, ll)


def energy_kernel(grads_ref, out_ref):
    x = grads_ref[...].astype(F32)
    out_ref[...] = jnp.full(out_ref.shape, jnp.sum(x * x))


def energy_call(grads):
    return pl.pallas_call(
        energy_kernel,
        out_shape=jax.ShapeDtypeStruct((8, 128), F32),
        in_specs=[pl.BlockSpec(memory_space=pltpu.VMEM)],
        out_specs=pl.BlockSpec(memory_space=pltpu.VMEM),
        compiler_params=pltpu.CompilerParams(vmem_limit_bytes=4 << 20),
        cost_estimate=pl.CostEstimate(flops=1 << 19, bytes_accessed=1 << 19, transcendentals=0),
        name="energy",
    )(grads)


def route_kernel(slots_ref, own_ref, other_ref, energy_ref, out_ref, source_ref):
    chips, rows = own_ref.shape[0], own_ref.shape[1]
    core = lax.rem(lax.axis_index("shard"), 2)
    for i in range(2 * chips):
        source_ref[slots_ref[0, i]] = i
    energy = energy_ref[...]
    high = energy.astype(BF16).astype(F32)
    middle = (energy - high).astype(BF16).astype(F32)
    low = energy - high - middle
    row = lax.broadcasted_iota(jnp.int32, energy.shape, 0)
    packed = jnp.where(row == 0, high, jnp.where(row == 1, middle, low)).astype(BF16)
    for chip in range(chips):
        block = source_ref[2 * chip + core]
        mine = lax.rem(block, 2) == core
        for part, high, wide in tiles(rows, own_ref.shape[2]):
            out_ref[chip, part, :] = jnp.where(mine, own_ref[block // 2, high, wide], other_ref[block // 2, high, wide])
        out_ref[chip, out_ref.shape[1] - 8 :, :] = packed


def return_kernel(slots_ref, own_ref, other_ref, out_ref):
    core = lax.rem(lax.axis_index("shard"), 2)
    for i in range(own_ref.shape[0]):
        slot = slots_ref[0, 2 * i + core]
        mine = lax.rem(slot, 2) == core
        out_ref[i] = jnp.where(mine, own_ref[slot // 2], other_ref[slot // 2])


def pick_call(kernel, shape, scratch, operands):
    return pl.pallas_call(
        kernel,
        out_shape=jax.ShapeDtypeStruct(shape, BF16),
        in_specs=[pl.BlockSpec(memory_space=pltpu.SMEM)]
        + [pl.BlockSpec(memory_space=pltpu.VMEM)] * (len(operands) - 1),
        out_specs=pl.BlockSpec(memory_space=pltpu.VMEM),
        scratch_shapes=scratch,
        compiler_params=pltpu.CompilerParams(vmem_limit_bytes=8 << 20),
        cost_estimate=pl.CostEstimate(flops=0, bytes_accessed=1 << 21, transcendentals=0),
    )(*operands)


def shards(grads, assignment, moment, second, left_stats, right_stats, left_basis, right_basis):
    shard_count = lax.axis_size("shard")
    tensor_count = lax.axis_size("tensor")
    size = grads.shape[1]
    chips = shard_count // 2
    rows = size // chips
    entries = float(size * size * shard_count * tensor_count)
    same_core = [[2 * p + q for p in range(chips)] for q in range(2)]
    swap = [(i, i ^ 1) for i in range(shard_count)]
    moment, second = moment[0], second[0]
    left_stats, right_stats = left_stats[0], right_stats[0]
    left_basis, right_basis = left_basis[0], right_basis[0]

    def exchange(pieces):
        return lax.all_to_all(pieces, "shard", 0, 0, axis_index_groups=same_core)

    arrived = exchange(grads.reshape(chips, rows, size))
    energy = energy_call(grads)
    moved = [
        lax.ppermute(
            energy, "tensor", [(i, (i + s) % tensor_count) for i in range(tensor_count)]
        )
        for s in range(1, tensor_count)
    ]
    for part in moved:
        energy = energy + part
    energy = energy + lax.ppermute(energy, "shard", swap)
    other = lax.ppermute(arrived, "shard", swap)
    routed = pick_call(
        route_kernel,
        (chips, rows * size // 128 + 8, 128),
        [pltpu.SMEM((shard_count,), jnp.int32)],
        (assignment, arrived, other, energy),
    )
    got = exchange(routed)
    left_half, turned, *halves = early_call(left_basis, left_stats, right_basis, moment)
    update, second_new, factor = step_call(entries, got, halves, turned, second)
    returned = exchange(update)
    right_basis_new = right_call(right_stats, right_basis)
    other = lax.ppermute(returned, "shard", swap)
    picked = pick_call(return_kernel, (chips, rows, size), [], (assignment, returned, other))
    update_out = exchange(picked).reshape(size, size)
    left_basis_new, moment_new, left_new, right_new = late_call(left_half, got, factor, moment, left_stats, right_stats)

    states = (moment_new, second_new, left_new, right_new, left_basis_new, right_basis_new)
    return (update_out,) + tuple(state[None] for state in states)


def solution(mesh):
    weights = P("shard", "tensor")
    state = P("shard", "tensor", None)

    return jax.shard_map(
        shards,
        mesh=mesh,
        in_specs=(weights, P("tensor", None)) + (state,) * 6,
        out_specs=(weights,) + (state,) * 6,
        check_vma=False,
    )
```

```python
import functools
import jax
import jax.numpy as jnp
from jax import lax
from jax.experimental import pallas as pl
from jax.experimental.pallas import tpu as pltpu
from jax.sharding import PartitionSpec as P


NS_ITERS = 2
BETA_MOMENT = 0.9
BETA_SECOND = 0.9
BETA_STATS = 0.9
ADAM_EPSILON = 1e-08
CLIP_RMS = 1.0
QUINTIC_A = 3.4445
QUINTIC_B = -4.775
QUINTIC_C = 2.0315
F32, BF16 = jnp.float32, jnp.bfloat16
NN = (((1,), (0,)), ((), ()))
NT = (((1,), (1,)), ((), ()))
BLK = 256


def mxu(a, b, dims=NN):
    return lax.dot_general(a, b, dims, preferred_element_type=F32)


def split(x):
    high = x.astype(BF16)
    return high, (x - high.astype(F32)).astype(BF16)


def store_split(x, high_ref, low_ref, at=slice(None)):
    high, low = split(x)
    high_ref[at, :] = high
    low_ref[at, :] = low


def blocks(ref, n=None):
    n = ref.shape[0]
    return [pl.ds(i, BLK) for i in range(0, n, BLK)]


def prod3(ah, al, bh, bl, at, dims=NN):
    a_high = ah[at, :]
    return mxu(a_high, bh[...], dims) + (mxu(a_high, bl[...], dims) + mxu(al[at, :], bh[...], dims))


def polynomial(y, ah, al, xh, xl, gh, gl):
    store_split(y[...], xh, xl)
    for at in blocks(y):
        store_split(prod3(xh, xl, xh, xl, at, NT), gh, gl, at)
    for at in blocks(y):
        square = prod3(gh, gl, gh, gl, at)
        gram = gh[at, :].astype(F32) + gl[at, :].astype(F32)
        store_split(QUINTIC_B * gram + QUINTIC_C * square, ah, al, at)


def sweep(y, ah, al, xh, xl, gh, gl):
    polynomial(y, ah, al, xh, xl, gh, gl)
    for at in blocks(y):
        y[at, :] = QUINTIC_A * y[at, :] + prod3(ah, al, xh, xl, at)


def last_sweep(y, ah, al, xh, xl, gh, gl, out, out_hbm, stores):
    polynomial(y, ah, al, xh, xl, gh, gl)
    gh[...] = xh[...].T
    gl[...] = xl[...].T
    before = None
    for at in blocks(y):
        rows = gh[at, :].astype(F32) + gl[at, :].astype(F32)
        out[at, :] = QUINTIC_A * rows + prod3(gh, gl, ah, al, at)
        if before is not None:
            stores.add(out.at[before, :], out_hbm.at[before, :])
        before = at
    stores.add(out.at[before, :], out_hbm.at[before, :])


def make_loads(pairs, sems):
    return [pltpu.make_async_copy(source, target, sems.at[i]) for i, (source, target) in enumerate(pairs)]


class Stores:
    def __init__(self, sems):
        self.sems, self.copies = sems, []

    def add(self, source, target):
        copy = pltpu.make_async_copy(source, target, self.sems.at[len(self.copies)])
        copy.start()
        self.copies.append(copy)

    def wait(self):
        for copy in self.copies:
            copy.wait()


def first_iterate(y, ah, al, bth, btl):
    total = jnp.zeros((), F32)
    for at in blocks(y):
        part = prod3(bth, btl, ah, al, at, NT)
        y[at, :] = part
        total = total + jnp.sum(part * part)
    y[...] = y[...] * lax.rsqrt(total + 1e-12)


def early_kernel(left_hbm, stats_hbm, right_hbm, moment_hbm,
                 y_hbm, pmq_hbm, lth_hbm, ltl_hbm, lh_hbm, ll_hbm, rh_hbm, rl_hbm,
                 left, stats, right, moment, y, pmq, lth, ltl, lh, ll, rh, rl, ah, al, xh, xl, gh, gl,
                 in_sems, out_sems):
    pairs = ((left_hbm, left), (stats_hbm, stats), (right_hbm, right), (moment_hbm, moment))
    loads = make_loads(pairs, in_sems)
    stores = Stores(out_sems)
    loads[0].start()
    loads[1].start()
    loads[0].wait()
    store_split(left[...].T, lth, ltl)
    loads[1].wait()
    loads[2].start()
    loads[3].start()
    store_split(stats[...], ah, al)
    first_iterate(y, ah, al, lth, ltl)
    store_split(left[...], lh, ll)
    for source, target in ((lth, lth_hbm), (ltl, ltl_hbm), (lh, lh_hbm), (ll, ll_hbm)):
        stores.add(source, target)
    sweep(y, ah, al, xh, xl, gh, gl)
    loads[2].wait()
    store_split(right[...], rh, rl)
    stores.add(y, y_hbm)
    loads[3].wait()
    store_split(moment[...], xh, xl)
    stores.add(rh, rh_hbm)
    stores.add(rl, rl_hbm)
    before = None
    for at in blocks(pmq):
        high, low = split(prod3(lth, ltl, xh, xl, at))
        if before is not None:
            stores.add(pmq.at[before, :], pmq_hbm.at[before, :])
        pmq[at, :] = mxu(high, rh[...]) + (mxu(high, rl[...]) + mxu(low, rh[...]))
        before = at
    stores.add(pmq.at[before, :], pmq_hbm.at[before, :])
    stores.wait()


def right_kernel(basis, stats_hbm, out_hbm, stats, y, ah, al, xh, xl, gh, gl, in_sems, out_sems):
    loads = make_loads(((stats_hbm, stats),), in_sems)
    stores = Stores(out_sems)
    loads[0].start()
    store_split(basis[...].T, xh, xl)
    loads[0].wait()
    store_split(stats[...], ah, al)
    first_iterate(y, ah, al, xh, xl)
    for _ in range(NS_ITERS - 1):
        sweep(y, ah, al, xh, xl, gh, gl)
    last_sweep(y, ah, al, xh, xl, gh, gl, stats, out_hbm, stores)
    stores.wait()


def late_kernel(y_hbm, got_hbm, factor_hbm, moment_hbm, left_hbm, right_hbm,
                basis_hbm, moment_out, left_out, right_out,
                y, got, factor_ref, moment, left, right, tile_ref, turned, out, ah, al, xh, xl, gh, gl,
                in_sems, out_sems):
    n, rows = moment.shape[0], tile_ref.shape[1]
    pairs = ((y_hbm, y), (got_hbm, got), (factor_hbm, factor_ref))
    pairs += ((moment_hbm, moment), (left_hbm, left), (right_hbm, right))
    loads = make_loads(pairs, in_sems)
    stores = Stores(out_sems)
    loads[0].start()
    loads[0].wait()
    for load in loads[1:]:
        load.start()
    last_sweep(y, ah, al, xh, xl, gh, gl, out, basis_hbm, stores)
    for load in loads[1:]:
        load.wait()
    for part, high, wide in tiles(rows, n):
        tile_ref[:, high, wide] = got[:, part, :]
    tile = tile_ref[...].reshape(n, n)
    turned[...] = tile.T
    factor = factor_ref[0:1, 0:1]
    scale = (1.0 - BETA_STATS) * factor * factor / n
    before = None
    for at in blocks(moment):
        mine = tile[at.start : at.start + BLK, :]
        moment[at, :] = BETA_MOMENT * moment[at, :] + (1.0 - BETA_MOMENT) * (factor * mine.astype(F32))
        left[at, :] = BETA_STATS * left[at, :] + scale * mxu(mine, tile, NT)
        right[at, :] = BETA_STATS * right[at, :] + scale * mxu(turned[at, :], tile)
        for part in (before, at if at.start + BLK == n else None):
            if part is not None:
                for source, target in ((moment, moment_out), (left, left_out), (right, right_out)):
                    stores.add(source.at[part, :], target.at[part, :])
        before = at
    stores.wait()


def window_call(kernel, operands, outs, scratch, passes, limit, ready=0):
    hbm = pl.BlockSpec(memory_space=pltpu.HBM)
    n = outs[0].shape[0]
    return pl.pallas_call(
        kernel,
        out_shape=outs,
        in_specs=[pl.BlockSpec(memory_space=pltpu.VMEM)] * ready + [hbm] * (len(operands) - ready),
        out_specs=[hbm] * len(outs),
        scratch_shapes=scratch + [pltpu.SemaphoreType.DMA((8,)), pltpu.SemaphoreType.DMA((12,))],
        compiler_params=pltpu.CompilerParams(vmem_limit_bytes=limit),
        cost_estimate=pl.CostEstimate(flops=2 * n**3 * passes, bytes_accessed=8 << 20, transcendentals=0),
    )(*operands)


def early_call(left, stats, right, moment):
    n = left.shape[0]
    full, half = (n, n), pltpu.VMEM((n, n), BF16)
    outs = (jax.ShapeDtypeStruct(full, F32),) * 2 + (jax.ShapeDtypeStruct(full, BF16),) * 6
    scratch = [pltpu.VMEM(full, F32)] * 6 + [half] * 12
    return window_call(early_kernel, (left, stats, right, moment), outs, scratch, 18, 65_600_000)


def right_call(stats, basis):
    n = stats.shape[0]
    scratch = [pltpu.VMEM((n, n), F32)] * 2 + [pltpu.VMEM((n, n), BF16)] * 6
    outs = (jax.ShapeDtypeStruct((n, n), F32),)
    return window_call(right_kernel, (basis, stats), outs, scratch, 21, 55_000_000, ready=1)[0]


def late_call(half, got, factor, moment, left, right):
    n = half.shape[0]
    full = pltpu.VMEM((n, n), F32)
    scratch = [full, pltpu.VMEM(got.shape, BF16), pltpu.VMEM(factor.shape, F32)] + [full] * 3
    scratch += [pltpu.VMEM((got.shape[0], n // got.shape[0], n), BF16), pltpu.VMEM((n, n), BF16), full]
    scratch += [pltpu.VMEM((n, n), BF16)] * 6
    outs = (jax.ShapeDtypeStruct((n, n), F32),) * 4
    return window_call(late_kernel, (half, got, factor, moment, left, right), outs, scratch, 11, 65_600_000)


def tiles(rows, n):
    across = n // 128
    return [
        (pl.ds((high * across + wide) * 16, 16), pl.ds(high * 16, 16), pl.ds(wide * 128, 128))
        for high in range(rows // 16)
        for wide in range(across)
    ]


def step_kernel(entries, got_hbm, lth_hbm, ltl_hbm, rh_hbm, rl_hbm, second_hbm, pmq_hbm, lh_hbm, ll_hbm,
                update_hbm, second_out_hbm, factor_ref,
                got_ref, tile_ref, lth, ltl, rh, rl, second_ref, pmq_ref, lh, ll, dh, dl, update_ref,
                in_sems, out_sems):
    pieces, rows = update_ref.shape[0], update_ref.shape[1]
    n = pieces * rows
    pairs = [(got_hbm, got_ref), (lth_hbm, lth), (ltl_hbm, ltl)]
    pairs += [(rh_hbm, rh), (rl_hbm, rl), (second_hbm, second_ref), (pmq_hbm, pmq_ref), (lh_hbm, lh), (ll_hbm, ll)]
    loads = [pltpu.make_async_copy(source, target, in_sems.at[i]) for i, (source, target) in enumerate(pairs)]
    for load in loads:
        load.start()
    loads[0].wait()
    for part, high, wide in tiles(rows, n):
        tile_ref[:, high, wide] = got_ref[:, part, :]
    for load in loads[1:3]:
        load.wait()
    packed = jnp.sum(got_ref[:, rows * n // 128 :, :].astype(F32), axis=0)
    energy = packed[0:1, 0:1] + packed[1:2, 0:1] + packed[2:3, 0:1]
    factor = jnp.minimum(1.0, CLIP_RMS / jnp.sqrt(energy / entries + 1e-12))
    factor_ref[...] = jnp.broadcast_to(factor, factor_ref.shape)
    tile = tile_ref[...].reshape(n, n)
    for i, at in enumerate(blocks(lth)):
        high, low = split(mxu(lth[at, :], tile) + mxu(ltl[at, :], tile))
        if i == 0:
            for load in loads[3:5]:
                load.wait()
        turned = mxu(high, rh[...]) + (mxu(high, rl[...]) + mxu(low, rh[...]))
        if i == 0:
            for load in loads[5:7]:
                load.wait()
        rotated = factor * turned
        second = BETA_SECOND * second_ref[at, :] + (1.0 - BETA_SECOND) * rotated * rotated
        second_ref[at, :] = second
        rotated_moment = BETA_MOMENT * pmq_ref[at, :] + (1.0 - BETA_MOMENT) * rotated
        store_split(rotated_moment / (jnp.sqrt(second) + ADAM_EPSILON), dh, dl, at)
    for load in loads[7:]:
        load.wait()
    count = BLK // rows
    stores = []
    for i, at in enumerate(blocks(lth)):
        high, low = split(prod3(lh, ll, dh, dl, at))
        if i == 0:
            stores.append(pltpu.make_async_copy(second_ref, second_out_hbm, out_sems.at[0]))
            stores[-1].start()
        out = mxu(high, rh[...], NT) + (mxu(high, rl[...], NT) + mxu(low, rh[...], NT))
        if i > 0:
            stores.append(send_rows(update_ref, update_hbm, i - 1, count, out_sems))
        update_ref[i * count : (i + 1) * count] = out.astype(BF16).reshape(count, rows, n)
    stores.append(send_rows(update_ref, update_hbm, n // BLK - 1, count, out_sems))
    for store in stores:
        store.wait()


def send_rows(source, target, i, count, sems):
    part = pl.ds(i * count, count)
    copy = pltpu.make_async_copy(source.at[part], target.at[part], sems.at[i + 1])
    copy.start()
    return copy


def step_call(entries, got, halves, pmq, second):
    n = pmq.shape[0]
    pieces = got.shape[0]
    lth, ltl, lh, ll, rh, rl = halves
    half, full = pltpu.VMEM((n, n), BF16), pltpu.VMEM((n, n), F32)
    hbm = pl.BlockSpec(memory_space=pltpu.HBM)
    vmem = pl.BlockSpec(memory_space=pltpu.VMEM)
    block = pltpu.VMEM((pieces, n // pieces, n), BF16)
    return pl.pallas_call(
        functools.partial(step_kernel, entries),
        out_shape=(
            jax.ShapeDtypeStruct((pieces, n // pieces, n), BF16),
            jax.ShapeDtypeStruct((n, n), F32),
            jax.ShapeDtypeStruct((8, 128), F32),
        ),
        in_specs=[hbm] * 9,
        out_specs=[hbm, hbm, vmem],
        scratch_shapes=[pltpu.VMEM(got.shape, BF16), block]
        + [half] * 4
        + [full] * 2
        + [half] * 4
        + [block, pltpu.SemaphoreType.DMA((9,)), pltpu.SemaphoreType.DMA((n // BLK + 1,))],
        compiler_params=pltpu.CompilerParams(vmem_limit_bytes=66_500_000),
        cost_estimate=pl.CostEstimate(flops=2 * n**3 * 11, bytes_accessed=7 << 20, transcendentals=0),
        name="step",
    )(got, lth, ltl, rh, rl, second, pmq, lh, ll)


def energy_kernel(grads_ref, out_ref):
    x = grads_ref[...].astype(F32)
    out_ref[...] = jnp.full(out_ref.shape, jnp.sum(x * x))


def energy_call(grads):
    return pl.pallas_call(
        energy_kernel,
        out_shape=jax.ShapeDtypeStruct((8, 128), F32),
        in_specs=[pl.BlockSpec(memory_space=pltpu.VMEM)],
        out_specs=pl.BlockSpec(memory_space=pltpu.VMEM),
        compiler_params=pltpu.CompilerParams(vmem_limit_bytes=4 << 20),
        cost_estimate=pl.CostEstimate(flops=1 << 19, bytes_accessed=1 << 19, transcendentals=0),
        name="energy",
    )(grads)


def route_kernel(slots_ref, own_ref, other_ref, energy_ref, out_ref, source_ref):
    chips, rows = own_ref.shape[0], own_ref.shape[1]
    core = lax.rem(lax.axis_index("shard"), 2)
    for i in range(2 * chips):
        source_ref[slots_ref[0, i]] = i
    energy = energy_ref[...]
    high = energy.astype(BF16).astype(F32)
    middle = (energy - high).astype(BF16).astype(F32)
    low = energy - high - middle
    row = lax.broadcasted_iota(jnp.int32, energy.shape, 0)
    packed = jnp.where(row == 0, high, jnp.where(row == 1, middle, low)).astype(BF16)
    for chip in range(chips):
        block = source_ref[2 * chip + core]
        mine = lax.rem(block, 2) == core
        for part, high, wide in tiles(rows, own_ref.shape[2]):
            out_ref[chip, part, :] = jnp.where(mine, own_ref[block // 2, high, wide], other_ref[block // 2, high, wide])
        out_ref[chip, out_ref.shape[1] - 8 :, :] = packed


def return_kernel(slots_ref, own_ref, other_ref, out_ref):
    core = lax.rem(lax.axis_index("shard"), 2)
    for i in range(own_ref.shape[0]):
        slot = slots_ref[0, 2 * i + core]
        mine = lax.rem(slot, 2) == core
        out_ref[i] = jnp.where(mine, own_ref[slot // 2], other_ref[slot // 2])


def pick_call(kernel, shape, scratch, operands):
    return pl.pallas_call(
        kernel,
        out_shape=jax.ShapeDtypeStruct(shape, BF16),
        in_specs=[pl.BlockSpec(memory_space=pltpu.SMEM)]
        + [pl.BlockSpec(memory_space=pltpu.VMEM)] * (len(operands) - 1),
        out_specs=pl.BlockSpec(memory_space=pltpu.VMEM),
        scratch_shapes=scratch,
        compiler_params=pltpu.CompilerParams(vmem_limit_bytes=8 << 20),
        cost_estimate=pl.CostEstimate(flops=0, bytes_accessed=1 << 21, transcendentals=0),
    )(*operands)


def shards(grads, assignment, moment, second, left_stats, right_stats, left_basis, right_basis):
    shard_count = lax.axis_size("shard")
    tensor_count = lax.axis_size("tensor")
    size = grads.shape[1]
    chips = shard_count // 2
    rows = size // chips
    entries = float(size * size * shard_count * tensor_count)
    same_core = [[2 * p + q for p in range(chips)] for q in range(2)]
    swap = [(i, i ^ 1) for i in range(shard_count)]
    moment, second = moment[0], second[0]
    left_stats, right_stats = left_stats[0], right_stats[0]
    left_basis, right_basis = left_basis[0], right_basis[0]

    def exchange(pieces):
        return lax.all_to_all(pieces, "shard", 0, 0, axis_index_groups=same_core)

    arrived = exchange(grads.reshape(chips, rows, size))
    energy = energy_call(grads)
    moved = [
        lax.ppermute(
            energy, "tensor", [(i, (i + s) % tensor_count) for i in range(tensor_count)]
        )
        for s in range(1, tensor_count)
    ]
    for part in moved:
        energy = energy + part
    energy = energy + lax.ppermute(energy, "shard", swap)
    other = lax.ppermute(arrived, "shard", swap)
    routed = pick_call(
        route_kernel,
        (chips, rows * size // 128 + 8, 128),
        [pltpu.SMEM((shard_count,), jnp.int32)],
        (assignment, arrived, other, energy),
    )
    got = exchange(routed)
    left_half, turned, *halves = early_call(left_basis, left_stats, right_basis, moment)
    update, second_new, factor = step_call(entries, got, halves, turned, second)
    returned = exchange(update)
    right_basis_new = right_call(right_stats, right_basis)
    other = lax.ppermute(returned, "shard", swap)
    picked = pick_call(return_kernel, (chips, rows, size), [], (assignment, returned, other))
    update_out = exchange(picked).reshape(size, size)
    left_basis_new, moment_new, left_new, right_new = late_call(left_half, got, factor, moment, left_stats, right_stats)

    states = (moment_new, second_new, left_new, right_new, left_basis_new, right_basis_new)
    return (update_out,) + tuple(state[None] for state in states)


def solution(mesh):
    weights = P("shard", "tensor")
    state = P("shard", "tensor", None)

    return jax.shard_map(
        shards,
        mesh=mesh,
        in_specs=(weights, P("tensor", None)) + (state,) * 6,
        out_specs=(weights,) + (state,) * 6,
        check_vma=False,
    )
```

```python
import functools
import jax
import jax.numpy as jnp
from jax import lax
from jax.experimental import pallas as pl
from jax.experimental.pallas import tpu as pltpu
from jax.sharding import PartitionSpec as P


NS_ITERS = 2
BETA_MOMENT = 0.9
BETA_SECOND = 0.9
BETA_STATS = 0.9
ADAM_EPSILON = 1e-08
CLIP_RMS = 1.0
QUINTIC_A = 3.4445
QUINTIC_B = -4.775
QUINTIC_C = 2.0315
F32, BF16 = jnp.float32, jnp.bfloat16
NN = (((1,), (0,)), ((), ()))
NT = (((1,), (1,)), ((), ()))
BLK = 256


def mxu(a, b, dims=NN):
    return lax.dot_general(a, b, dims, preferred_element_type=F32)


def split(x):
    high = x.astype(BF16)
    return high, (x - high.astype(F32)).astype(BF16)


def store_split(x, high_ref, low_ref, at=slice(None)):
    high, low = split(x)
    high_ref[at, :] = high
    low_ref[at, :] = low


def blocks(ref, n=None):
    n = ref.shape[0]
    return [pl.ds(i, BLK) for i in range(0, n, BLK)]


def prod3(ah, al, bh, bl, at, dims=NN):
    a_high = ah[at, :]
    return mxu(a_high, bh[...], dims) + (mxu(a_high, bl[...], dims) + mxu(al[at, :], bh[...], dims))


def polynomial(y, ah, al, xh, xl, gh, gl):
    store_split(y[...], xh, xl)
    for at in blocks(y):
        store_split(prod3(xh, xl, xh, xl, at, NT), gh, gl, at)
    for at in blocks(y):
        square = prod3(gh, gl, gh, gl, at)
        gram = gh[at, :].astype(F32) + gl[at, :].astype(F32)
        store_split(QUINTIC_B * gram + QUINTIC_C * square, ah, al, at)


def sweep(y, ah, al, xh, xl, gh, gl):
    polynomial(y, ah, al, xh, xl, gh, gl)
    for at in blocks(y):
        y[at, :] = QUINTIC_A * y[at, :] + prod3(ah, al, xh, xl, at)


def last_sweep(y, ah, al, xh, xl, gh, gl, out, out_hbm, stores):
    polynomial(y, ah, al, xh, xl, gh, gl)
    gh[...] = xh[...].T
    gl[...] = xl[...].T
    before = None
    for at in blocks(y):
        rows = gh[at, :].astype(F32) + gl[at, :].astype(F32)
        out[at, :] = QUINTIC_A * rows + prod3(gh, gl, ah, al, at)
        if before is not None:
            stores.add(out.at[before, :], out_hbm.at[before, :])
        before = at
    stores.add(out.at[before, :], out_hbm.at[before, :])


def make_loads(pairs, sems):
    return [pltpu.make_async_copy(source, target, sems.at[i]) for i, (source, target) in enumerate(pairs)]


class Stores:
    def __init__(self, sems):
        self.sems, self.copies = sems, []

    def add(self, source, target):
        copy = pltpu.make_async_copy(source, target, self.sems.at[len(self.copies)])
        copy.start()
        self.copies.append(copy)

    def wait(self):
        for copy in self.copies:
            copy.wait()


def first_iterate(y, ah, al, bth, btl):
    total = jnp.zeros((), F32)
    for at in blocks(y):
        part = prod3(bth, btl, ah, al, at, NT)
        y[at, :] = part
        total = total + jnp.sum(part * part)
    y[...] = y[...] * lax.rsqrt(total + 1e-12)


def early_kernel(left_hbm, stats_hbm, right_hbm, moment_hbm,
                 y_hbm, pmq_hbm, lth_hbm, ltl_hbm, lh_hbm, ll_hbm, rh_hbm, rl_hbm,
                 left, stats, right, moment, y, pmq, lth, ltl, lh, ll, rh, rl, ah, al, xh, xl, gh, gl,
                 in_sems, out_sems):
    pairs = ((left_hbm, left), (stats_hbm, stats), (right_hbm, right), (moment_hbm, moment))
    loads = make_loads(pairs, in_sems)
    stores = Stores(out_sems)
    loads[0].start()
    loads[1].start()
    loads[0].wait()
    store_split(left[...].T, lth, ltl)
    loads[1].wait()
    loads[2].start()
    loads[3].start()
    store_split(stats[...], ah, al)
    first_iterate(y, ah, al, lth, ltl)
    store_split(left[...], lh, ll)
    for source, target in ((lth, lth_hbm), (ltl, ltl_hbm), (lh, lh_hbm), (ll, ll_hbm)):
        stores.add(source, target)
    sweep(y, ah, al, xh, xl, gh, gl)
    loads[2].wait()
    store_split(right[...], rh, rl)
    stores.add(y, y_hbm)
    loads[3].wait()
    store_split(moment[...], xh, xl)
    stores.add(rh, rh_hbm)
    stores.add(rl, rl_hbm)
    before = None
    for at in blocks(pmq):
        high, low = split(prod3(lth, ltl, xh, xl, at))
        if before is not None:
            stores.add(pmq.at[before, :], pmq_hbm.at[before, :])
        pmq[at, :] = mxu(high, rh[...]) + (mxu(high, rl[...]) + mxu(low, rh[...]))
        before = at
    stores.add(pmq.at[before, :], pmq_hbm.at[before, :])
    stores.wait()


def right_kernel(basis, stats_hbm, out_hbm, stats, y, ah, al, xh, xl, gh, gl, in_sems, out_sems):
    loads = make_loads(((stats_hbm, stats),), in_sems)
    stores = Stores(out_sems)
    loads[0].start()
    store_split(basis[...].T, xh, xl)
    loads[0].wait()
    store_split(stats[...], ah, al)
    first_iterate(y, ah, al, xh, xl)
    for _ in range(NS_ITERS - 1):
        sweep(y, ah, al, xh, xl, gh, gl)
    last_sweep(y, ah, al, xh, xl, gh, gl, stats, out_hbm, stores)
    stores.wait()


def late_kernel(y_hbm, got_hbm, factor_hbm, moment_hbm, left_hbm, right_hbm,
                basis_hbm, moment_out, left_out, right_out,
                y, got, factor_ref, moment, left, right, tile_ref, turned, out, ah, al, xh, xl, gh, gl,
                in_sems, out_sems):
    n, rows = moment.shape[0], tile_ref.shape[1]
    pairs = ((y_hbm, y), (got_hbm, got), (factor_hbm, factor_ref))
    pairs += ((moment_hbm, moment), (left_hbm, left), (right_hbm, right))
    loads = make_loads(pairs, in_sems)
    stores = Stores(out_sems)
    loads[0].start()
    loads[0].wait()
    for load in loads[1:]:
        load.start()
    last_sweep(y, ah, al, xh, xl, gh, gl, out, basis_hbm, stores)
    for load in loads[1:]:
        load.wait()
    for part, high, wide in tiles(rows, n):
        tile_ref[:, high, wide] = got[:, part, :]
    tile = tile_ref[...].reshape(n, n)
    turned[...] = tile.T
    factor = factor_ref[0:1, 0:1]
    scale = (1.0 - BETA_STATS) * factor * factor / n
    before = None
    for at in blocks(moment):
        mine = tile[at.start : at.start + BLK, :]
        moment[at, :] = BETA_MOMENT * moment[at, :] + (1.0 - BETA_MOMENT) * (factor * mine.astype(F32))
        left[at, :] = BETA_STATS * left[at, :] + scale * mxu(mine, tile, NT)
        right[at, :] = BETA_STATS * right[at, :] + scale * mxu(turned[at, :], tile)
        for part in (before, at if at.start + BLK == n else None):
            if part is not None:
                for source, target in ((moment, moment_out), (left, left_out), (right, right_out)):
                    stores.add(source.at[part, :], target.at[part, :])
        before = at
    stores.wait()


def window_call(kernel, operands, outs, scratch, passes, limit, ready=0):
    hbm = pl.BlockSpec(memory_space=pltpu.HBM)
    n = outs[0].shape[0]
    return pl.pallas_call(
        kernel,
        out_shape=outs,
        in_specs=[pl.BlockSpec(memory_space=pltpu.VMEM)] * ready + [hbm] * (len(operands) - ready),
        out_specs=[hbm] * len(outs),
        scratch_shapes=scratch + [pltpu.SemaphoreType.DMA((8,)), pltpu.SemaphoreType.DMA((12,))],
        compiler_params=pltpu.CompilerParams(vmem_limit_bytes=limit),
        cost_estimate=pl.CostEstimate(flops=2 * n**3 * passes, bytes_accessed=8 << 20, transcendentals=0),
    )(*operands)


def early_call(left, stats, right, moment):
    n = left.shape[0]
    full, half = (n, n), pltpu.VMEM((n, n), BF16)
    outs = (jax.ShapeDtypeStruct(full, F32),) * 2 + (jax.ShapeDtypeStruct(full, BF16),) * 6
    scratch = [pltpu.VMEM(full, F32)] * 6 + [half] * 12
    return window_call(early_kernel, (left, stats, right, moment), outs, scratch, 18, 65_600_000)


def right_call(stats, basis):
    n = stats.shape[0]
    scratch = [pltpu.VMEM((n, n), F32)] * 2 + [pltpu.VMEM((n, n), BF16)] * 6
    outs = (jax.ShapeDtypeStruct((n, n), F32),)
    return window_call(right_kernel, (basis, stats), outs, scratch, 21, 55_000_000, ready=1)[0]


def late_call(half, got, factor, moment, left, right):
    n = half.shape[0]
    full = pltpu.VMEM((n, n), F32)
    scratch = [full, pltpu.VMEM(got.shape, BF16), pltpu.VMEM(factor.shape, F32)] + [full] * 3
    scratch += [pltpu.VMEM((got.shape[0], n // got.shape[0], n), BF16), pltpu.VMEM((n, n), BF16), full]
    scratch += [pltpu.VMEM((n, n), BF16)] * 6
    outs = (jax.ShapeDtypeStruct((n, n), F32),) * 4
    return window_call(late_kernel, (half, got, factor, moment, left, right), outs, scratch, 11, 65_600_000)


def tiles(rows, n):
    across = n // 128
    return [
        (pl.ds((high * across + wide) * 16, 16), pl.ds(high * 16, 16), pl.ds(wide * 128, 128))
        for high in range(rows // 16)
        for wide in range(across)
    ]


def step_kernel(entries, got_hbm, lth_hbm, ltl_hbm, rh_hbm, rl_hbm, second_hbm, pmq_hbm, lh_hbm, ll_hbm,
                update_hbm, second_out_hbm, factor_ref,
                got_ref, tile_ref, lth, ltl, rh, rl, second_ref, pmq_ref, lh, ll, dh, dl, update_ref,
                in_sems, out_sems):
    pieces, rows = update_ref.shape[0], update_ref.shape[1]
    n = pieces * rows
    pairs = [(got_hbm, got_ref), (lth_hbm, lth), (ltl_hbm, ltl)]
    pairs += [(rh_hbm, rh), (rl_hbm, rl), (second_hbm, second_ref), (pmq_hbm, pmq_ref), (lh_hbm, lh), (ll_hbm, ll)]
    loads = [pltpu.make_async_copy(source, target, in_sems.at[i]) for i, (source, target) in enumerate(pairs)]
    for load in loads:
        load.start()
    loads[0].wait()
    for part, high, wide in tiles(rows, n):
        tile_ref[:, high, wide] = got_ref[:, part, :]
    for load in loads[1:3]:
        load.wait()
    packed = jnp.sum(got_ref[:, rows * n // 128 :, :].astype(F32), axis=0)
    energy = packed[0:1, 0:1] + packed[1:2, 0:1] + packed[2:3, 0:1]
    factor = jnp.minimum(1.0, CLIP_RMS / jnp.sqrt(energy / entries + 1e-12))
    factor_ref[...] = jnp.broadcast_to(factor, factor_ref.shape)
    tile = tile_ref[...].reshape(n, n)
    for i, at in enumerate(blocks(lth)):
        high, low = split(mxu(lth[at, :], tile) + mxu(ltl[at, :], tile))
        if i == 0:
            for load in loads[3:5]:
                load.wait()
        turned = mxu(high, rh[...]) + (mxu(high, rl[...]) + mxu(low, rh[...]))
        if i == 0:
            for load in loads[5:7]:
                load.wait()
        rotated = factor * turned
        second = BETA_SECOND * second_ref[at, :] + (1.0 - BETA_SECOND) * rotated * rotated
        second_ref[at, :] = second
        rotated_moment = BETA_MOMENT * pmq_ref[at, :] + (1.0 - BETA_MOMENT) * rotated
        store_split(rotated_moment / (jnp.sqrt(second) + ADAM_EPSILON), dh, dl, at)
    for load in loads[7:]:
        load.wait()
    count = BLK // rows
    stores = []
    for i, at in enumerate(blocks(lth)):
        high, low = split(prod3(lh, ll, dh, dl, at))
        if i == 0:
            stores.append(pltpu.make_async_copy(second_ref, second_out_hbm, out_sems.at[0]))
            stores[-1].start()
        out = mxu(high, rh[...], NT) + (mxu(high, rl[...], NT) + mxu(low, rh[...], NT))
        if i > 0:
            stores.append(send_rows(update_ref, update_hbm, i - 1, count, out_sems))
        update_ref[i * count : (i + 1) * count] = out.astype(BF16).reshape(count, rows, n)
    stores.append(send_rows(update_ref, update_hbm, n // BLK - 1, count, out_sems))
    for store in stores:
        store.wait()


def send_rows(source, target, i, count, sems):
    part = pl.ds(i * count, count)
    copy = pltpu.make_async_copy(source.at[part], target.at[part], sems.at[i + 1])
    copy.start()
    return copy


def step_call(entries, got, halves, pmq, second):
    n = pmq.shape[0]
    pieces = got.shape[0]
    lth, ltl, lh, ll, rh, rl = halves
    half, full = pltpu.VMEM((n, n), BF16), pltpu.VMEM((n, n), F32)
    hbm = pl.BlockSpec(memory_space=pltpu.HBM)
    vmem = pl.BlockSpec(memory_space=pltpu.VMEM)
    block = pltpu.VMEM((pieces, n // pieces, n), BF16)
    return pl.pallas_call(
        functools.partial(step_kernel, entries),
        out_shape=(
            jax.ShapeDtypeStruct((pieces, n // pieces, n), BF16),
            jax.ShapeDtypeStruct((n, n), F32),
            jax.ShapeDtypeStruct((8, 128), F32),
        ),
        in_specs=[hbm] * 9,
        out_specs=[hbm, hbm, vmem],
        scratch_shapes=[pltpu.VMEM(got.shape, BF16), block]
        + [half] * 4
        + [full] * 2
        + [half] * 4
        + [block, pltpu.SemaphoreType.DMA((9,)), pltpu.SemaphoreType.DMA((n // BLK + 1,))],
        compiler_params=pltpu.CompilerParams(vmem_limit_bytes=66_500_000),
        cost_estimate=pl.CostEstimate(flops=2 * n**3 * 11, bytes_accessed=7 << 20, transcendentals=0),
        name="step",
    )(got, lth, ltl, rh, rl, second, pmq, lh, ll)


def energy_kernel(grads_ref, out_ref):
    x = grads_ref[...].astype(F32)
    out_ref[...] = jnp.full(out_ref.shape, jnp.sum(x * x))


def energy_call(grads):
    return pl.pallas_call(
        energy_kernel,
        out_shape=jax.ShapeDtypeStruct((8, 128), F32),
        in_specs=[pl.BlockSpec(memory_space=pltpu.VMEM)],
        out_specs=pl.BlockSpec(memory_space=pltpu.VMEM),
        compiler_params=pltpu.CompilerParams(vmem_limit_bytes=4 << 20),
        cost_estimate=pl.CostEstimate(flops=1 << 19, bytes_accessed=1 << 19, transcendentals=0),
        name="energy",
    )(grads)


def route_kernel(slots_ref, own_ref, other_ref, energy_ref, out_ref, source_ref):
    chips, rows = own_ref.shape[0], own_ref.shape[1]
    core = lax.rem(lax.axis_index("shard"), 2)
    for i in range(2 * chips):
        source_ref[slots_ref[0, i]] = i
    energy = energy_ref[...]
    high = energy.astype(BF16).astype(F32)
    middle = (energy - high).astype(BF16).astype(F32)
    low = energy - high - middle
    row = lax.broadcasted_iota(jnp.int32, energy.shape, 0)
    packed = jnp.where(row == 0, high, jnp.where(row == 1, middle, low)).astype(BF16)
    for chip in range(chips):
        block = source_ref[2 * chip + core]
        mine = lax.rem(block, 2) == core
        for part, high, wide in tiles(rows, own_ref.shape[2]):
            out_ref[chip, part, :] = jnp.where(mine, own_ref[block // 2, high, wide], other_ref[block // 2, high, wide])
        out_ref[chip, out_ref.shape[1] - 8 :, :] = packed


def return_kernel(slots_ref, own_ref, other_ref, out_ref, sems):
    core = lax.rem(lax.axis_index("shard"), 2)
    for i in range(own_ref.shape[0]):
        slot = slots_ref[0, 2 * i + core]
        mine = lax.rem(slot, 2) == core

        @pl.when(mine)
        def _():
            pltpu.make_async_copy(own_ref.at[slot // 2], out_ref.at[i], sems.at[i]).start()

        @pl.when(jnp.logical_not(mine))
        def _():
            pltpu.make_async_copy(other_ref.at[slot // 2], out_ref.at[i], sems.at[i]).start()

    for i in range(own_ref.shape[0]):
        pltpu.make_async_copy(own_ref.at[i], out_ref.at[i], sems.at[i]).wait()


def pick_call(kernel, shape, scratch, operands, space=pltpu.VMEM):
    return pl.pallas_call(
        kernel,
        out_shape=jax.ShapeDtypeStruct(shape, BF16),
        in_specs=[pl.BlockSpec(memory_space=pltpu.SMEM)]
        + [pl.BlockSpec(memory_space=pltpu.VMEM)] * (len(operands) - 1),
        out_specs=pl.BlockSpec(memory_space=space),
        scratch_shapes=scratch,
        compiler_params=pltpu.CompilerParams(vmem_limit_bytes=8 << 20),
        cost_estimate=pl.CostEstimate(flops=0, bytes_accessed=1 << 21, transcendentals=0),
    )(*operands)


def shards(grads, assignment, moment, second, left_stats, right_stats, left_basis, right_basis):
    shard_count = lax.axis_size("shard")
    tensor_count = lax.axis_size("tensor")
    size = grads.shape[1]
    chips = shard_count // 2
    rows = size // chips
    entries = float(size * size * shard_count * tensor_count)
    same_core = [[2 * p + q for p in range(chips)] for q in range(2)]
    swap = [(i, i ^ 1) for i in range(shard_count)]
    moment, second = moment[0], second[0]
    left_stats, right_stats = left_stats[0], right_stats[0]
    left_basis, right_basis = left_basis[0], right_basis[0]

    def exchange(pieces):
        return lax.all_to_all(pieces, "shard", 0, 0, axis_index_groups=same_core)

    arrived = exchange(grads.reshape(chips, rows, size))
    energy = energy_call(grads)
    moved = [
        lax.ppermute(
            energy, "tensor", [(i, (i + s) % tensor_count) for i in range(tensor_count)]
        )
        for s in range(1, tensor_count)
    ]
    for part in moved:
        energy = energy + part
    energy = energy + lax.ppermute(energy, "shard", swap)
    other = lax.ppermute(arrived, "shard", swap)
    routed = pick_call(
        route_kernel,
        (chips, rows * size // 128 + 8, 128),
        [pltpu.SMEM((shard_count,), jnp.int32)],
        (assignment, arrived, other, energy),
    )
    got = exchange(routed)
    left_half, turned, *halves = early_call(left_basis, left_stats, right_basis, moment)
    update, second_new, factor = step_call(entries, got, halves, turned, second)
    returned = exchange(update)
    right_basis_new = right_call(right_stats, right_basis)
    other = lax.ppermute(returned, "shard", swap)
    picked = pick_call(
        return_kernel,
        (chips, rows, size),
        [pltpu.SemaphoreType.DMA((chips,))],
        (assignment, returned, other),
        pltpu.HBM,
    )
    update_out = exchange(picked).reshape(size, size)
    left_basis_new, moment_new, left_new, right_new = late_call(left_half, got, factor, moment, left_stats, right_stats)

    states = (moment_new, second_new, left_new, right_new, left_basis_new, right_basis_new)
    return (update_out,) + tuple(state[None] for state in states)


def solution(mesh):
    weights = P("shard", "tensor")
    state = P("shard", "tensor", None)

    return jax.shard_map(
        shards,
        mesh=mesh,
        in_specs=(weights, P("tensor", None)) + (state,) * 6,
        out_specs=(weights,) + (state,) * 6,
        check_vma=False,
    )
```
